512 devices in a mesh: fsdp: 16 (over z_lo, core), tp: 32 (over x, y, z_hi).
Axes of the slice: x: 4, y: 4, z: 16 (z_hi: 2, z_lo: 8; z = z_hi * 8 + z_lo), core: 2. Of those that a mesh axis runs over, the one named last changes fastest.
Arguments:
- inputs: bfloat16 [128, 16, 8192], P('tp', None, 'fsdp'), may hold values from -6 to 6
- featurizer: bfloat16 [8192, 3, 8192], P('fsdp', None, 'tp'), may hold values from -0.0625 to 0.0625
- short_filter: float32 [3, 3, 8192], P(None, None, 'tp'), may hold values from -3 to 3
- long_filter: float32 [512, 128], P('tp'), may hold values from -1.2 to 1.2
- decay_rate: float32 [512], P('tp'), may hold values from 0.004 to 0.08
- skip_gain: float32 [8192], P('tp'), may hold values from -1 to 1
- output_grad: bfloat16 [128, 16, 8192], P(None, 'fsdp', 'tp'), may hold values from -6 to 6
Outputs:
- hyena_out: bfloat16 [128, 16, 8192], P(None, 'fsdp', 'tp')
- input_grad: bfloat16 [128, 16, 8192], P('tp', None, 'fsdp')
- weight_grad: bfloat16 [8192, 3, 8192], P('fsdp', None, 'tp')
The draws below stay inside these ranges and needn't reach their ends.
All inputs are finite; a program needn't handle non-finite values.
Results may differ from the reference program's by a relative error of at most 0.028.
Values may be sent and summed in bfloat16 or wider, within the bound.
No kernel may reach another device: no remote copies, remote signals or barrier semaphores. Data moves between devices by JAX's collectives and lax.ppermute only.
A program may use at most 64 MiB of HBM per device.

```python
import math
import jax
import jax.numpy as jnp
from jax import lax

D = 8192
HC = 8192
CH_GROUP = 16
FILT_LEN = 128
SHORT_LEN = 3
TOK = 128
BLOCKS = 16
SEQ_LEN = 2048
FILTERS = 512
N_TP = 32


def level_of(key, shape, split, smallest, high):
    def one(axis_at, shards_of):
        steps = jax.random.uniform(jax.random.fold_in(jax.random.fold_in(key, 6), axis_at), (shards_of,), jnp.float32, smallest / len(split), high / len(split))
        return jnp.repeat(jnp.exp(steps), shape[axis_at] // shards_of).reshape((-1,) + (1,) * (len(shape) - axis_at - 1))

    gain = one(*split[0])
    for cut in split[1:]:
        gain = gain * one(*cut)
    return gain


def bell_draw(own_key, extent, scale, limit, pieces=(), kind=jnp.bfloat16):
    entries = jax.random.normal(own_key, extent, jnp.float32) * scale
    if len(pieces) > 0:
        entries = level_of(own_key, extent, pieces, -0.22, 0.18) * entries
    return jnp.clip(entries, min=-limit, max=limit).astype(kind)


def setup_inputs(seed: int = 0) -> dict:
    arg_keys = jax.random.split(jax.random.key(seed), 8)
    return {
        "inputs": bell_draw(arg_keys[0], (TOK, BLOCKS, D), 1.0, 6.0, ((0, 32), (2, 16))),
        "featurizer": bell_draw(arg_keys[1], (D, 3, HC), D ** -0.5, 0.0625, ((0, 16), (2, 32))),
        "short_filter": bell_draw(arg_keys[2], (SHORT_LEN, 3, HC), 0.6, 3.0, ((2, 32),), jnp.float32),
        "long_filter": bell_draw(arg_keys[3], (FILTERS, FILT_LEN), 0.2, 1.2, ((0, 32),), jnp.float32),
        "decay_rate": jnp.clip(jnp.exp(math.log(0.08) - 2.9957322 * jax.random.uniform(arg_keys[4], (FILTERS,), jnp.float32) ** level_of(arg_keys[4], (FILTERS,), ((0, 32),), -0.2, 0.2)), 0.004, 0.08),
        "skip_gain": jnp.clip(jax.random.uniform(arg_keys[5], (HC,), jnp.float32, -1.0, 1.0) * level_of(arg_keys[5], (HC,), ((0, 32),), -0.4, 0.0), -1.0, 1.0),
        "output_grad": bell_draw(arg_keys[6], (TOK, BLOCKS, HC), 1.0, 6.0, ((1, 16), (2, 32))),
    }


def delayed(values, steps):
    if steps == 0:
        return values
    padding = jnp.zeros((steps,) + values.shape[1:], values.dtype)
    return jnp.concatenate([padding, values[:values.shape[0] - steps]], 0)


def advanced(values, steps):
    if steps == 0:
        return values
    padding = jnp.zeros((steps,) + values.shape[1:], values.dtype)
    return jnp.concatenate([values[steps:], padding], 0)


def toeplitz_pair(kernel, tokens):
    tap_count = kernel.shape[1]
    positions = jnp.arange(tokens).astype(jnp.int32)
    lag_grid = positions[:, None] - positions[None, :]
    near_inside = (lag_grid >= 0) & (lag_grid < tap_count)
    near_taken = jnp.take(kernel, jnp.clip(lag_grid, 0, tap_count - 1).astype(jnp.int32), axis=1)
    near_matrix = jnp.where(near_inside[None], near_taken, jnp.zeros_like(near_taken))
    far_grid = lag_grid + tokens
    far_inside = far_grid < tap_count
    far_taken = jnp.take(kernel, jnp.clip(far_grid, 0, tap_count - 1).astype(jnp.int32), axis=1)
    far_matrix = jnp.where(far_inside[None], far_taken, jnp.zeros_like(far_taken))
    return near_matrix, far_matrix


def hyena_layer(features, short_filter, long_filter, decay_rate, skip_gain, output_grad):
    feat_wide = features.astype(jnp.float32)
    filtered = short_filter[0] * feat_wide
    for lag_step in range(1, SHORT_LEN):
        filtered = filtered + short_filter[lag_step] * delayed(feat_wide, lag_step)
    queries = filtered[:, 0]
    key_part = filtered[:, 1]
    value_part = filtered[:, 2]
    product = key_part * value_part
    offsets = jnp.arange(FILT_LEN).astype(jnp.float32)
    kernel = long_filter * jnp.exp(-decay_rate[:, None] * offsets[None, :])
    near_matrix, far_matrix = toeplitz_pair(kernel, TOK)
    grouped = product.reshape(BLOCKS, TOK, FILTERS, CH_GROUP)
    earlier = delayed(grouped, 1)
    convolved = jnp.einsum("nst,btnc->bsnc", near_matrix, grouped, precision=lax.Precision.HIGHEST)
    convolved = convolved + jnp.einsum("nst,btnc->bsnc", far_matrix, earlier, precision=lax.Precision.HIGHEST)
    convolved = convolved.reshape(SEQ_LEN, HC) + skip_gain * product
    output = (queries * convolved).astype(jnp.bfloat16)
    upstream = output_grad.astype(jnp.float32)
    query_grad = upstream * convolved
    conv_grad = upstream * queries
    conv_grouped = conv_grad.reshape(BLOCKS, TOK, FILTERS, CH_GROUP)
    later_grad = advanced(conv_grouped, 1)
    product_grad = jnp.einsum("nst,bsnc->btnc", near_matrix, conv_grouped, precision=lax.Precision.HIGHEST)
    product_grad = product_grad + jnp.einsum("nst,bsnc->btnc", far_matrix, later_grad, precision=lax.Precision.HIGHEST)
    product_grad = product_grad.reshape(SEQ_LEN, HC) + skip_gain * conv_grad
    filtered_grad = jnp.stack([query_grad, product_grad * value_part, product_grad * key_part], axis=1)
    feature_grad = short_filter[0] * filtered_grad
    for lag_step in range(1, SHORT_LEN):
        feature_grad = feature_grad + short_filter[lag_step] * advanced(filtered_grad, lag_step)
    return output, feature_grad.astype(jnp.bfloat16)


def reference(inputs, featurizer, short_filter, long_filter, decay_rate, skip_gain, output_grad):
    flat_inputs = inputs.reshape(TOK * BLOCKS, D)
    features = jnp.dot(flat_inputs, featurizer.reshape(D, 3 * HC), preferred_element_type=jnp.float32)
    features = features.astype(jnp.bfloat16).reshape(TOK, BLOCKS, 3, HC)
    seq_features = features.transpose(1, 0, 2, 3).reshape(SEQ_LEN, 3, HC)
    seq_grad = output_grad.transpose(1, 0, 2).reshape(SEQ_LEN, HC)
    seq_output, seq_feature_grad = hyena_layer(seq_features, short_filter, long_filter, decay_rate, skip_gain, seq_grad)
    hyena_out = seq_output.reshape(BLOCKS, TOK, HC).transpose(1, 0, 2)
    feature_grad = seq_feature_grad.reshape(BLOCKS, TOK, 3, HC).transpose(1, 0, 2, 3)
    weight_grad = lax.dot_general(inputs, feature_grad, (((0, 1), (0, 1)), ((), ())), preferred_element_type=jnp.float32)
    weight_grad = weight_grad.astype(jnp.bfloat16)
    slab_width = HC // N_TP
    grad_blocks = feature_grad.reshape(TOK * BLOCKS, 3, N_TP, slab_width).transpose(2, 0, 1, 3).reshape(N_TP, TOK * BLOCKS, 3 * slab_width)
    weight_blocks = featurizer.reshape(D, 3, N_TP, slab_width).transpose(2, 0, 1, 3).reshape(N_TP, D, 3 * slab_width)

    def add_slab(running, operands):
        partial_value = lax.dot_general(operands[0], operands[1], (((1,), (1,)), ((), ())), preferred_element_type=jnp.float32)
        rounded = lax.optimization_barrier(partial_value.astype(jnp.bfloat16))
        return running + rounded.astype(jnp.float32), None

    running, unused = lax.scan(add_slab, jnp.zeros((TOK * BLOCKS, D), jnp.float32), (grad_blocks, weight_blocks))
    input_grad = running.astype(jnp.bfloat16).reshape(TOK, BLOCKS, D)
    return hyena_out, input_grad, weight_grad
```

```python
import functools
import math

import jax
import jax.numpy as jnp
from jax import lax
from jax.experimental import pallas as pl
from jax.experimental.pallas import tpu as pltpu
from jax.sharding import Mesh
from jax.sharding import PartitionSpec as P

F32 = jnp.float32
BF16 = jnp.bfloat16
INTERPRET = False


def call(body, outs, *args, scratch=()):
    whole = pl.BlockSpec(memory_space=pltpu.VMEM)
    many = isinstance(outs, (tuple, list))
    size = sum(math.prod(a.shape) * a.dtype.itemsize for a in args)
    return pl.pallas_call(
        body,
        out_shape=outs,
        in_specs=[whole] * len(args),
        out_specs=[whole] * len(outs) if many else whole,
        scratch_shapes=list(scratch),
        cost_estimate=pl.CostEstimate(flops=10**9, bytes_accessed=size, transcendentals=0),
        interpret=INTERPRET,
    )(*args)


def shape(dims, kind):
    return jax.ShapeDtypeStruct(dims, kind)


def dot(a, b):
    return jnp.dot(a, b, preferred_element_type=F32)


def dot_nt(a, b):
    return lax.dot_general(a, b, (((1,), (1,)), ((), ())), preferred_element_type=F32)


def bit_reversed(count):
    bits = count.bit_length() - 1
    return [int(format(i, f"0{bits}b")[::-1], 2) if bits else 0 for i in range(count)]


def row_order(pieces, members, tokens, inverse):
    rows = pieces * members * tokens
    r = lax.broadcasted_iota(jnp.int32, (rows, rows), 0)
    c = lax.broadcasted_iota(jnp.int32, (rows, rows), 1)
    if inverse:
        r, c = c, r
    member, rest = r // (pieces * tokens), r % (pieces * tokens)
    piece, token = rest // tokens, rest % tokens
    return jnp.where(c == (piece * members + member) * tokens + token, 1.0, 0.0).astype(BF16)


def token_order(half, tokens, count, inverse):
    r = lax.broadcasted_iota(jnp.int32, (count, count), 0)
    c = lax.broadcasted_iota(jnp.int32, (count, count), 1)
    if inverse:
        r, c = c, r
    piece, rest = r // (2 * tokens), r % (2 * tokens)
    side, token = rest // tokens, rest % tokens
    relative = jnp.where(side == half, 0, 1)
    return jnp.where(c == relative * (count // 2) + piece * tokens + token, 1.0, 0.0).astype(BF16)


def toeplitz_body(taps_ref, rev_ref, decay_ref, fwd_ref, bwd_ref):
    filters, taps = taps_ref.shape
    lag = lax.broadcasted_iota(jnp.int32, (1, taps), 1)
    back = jnp.where(lag == 0, 0, taps - lag)
    row = lax.broadcasted_iota(jnp.int32, (taps, taps), 0)
    col = lax.broadcasted_iota(jnp.int32, (taps, taps), 1)
    for n in range(filters):
        rate = -decay_ref[n : n + 1, :]
        plain = taps_ref[n : n + 1, :] * jnp.exp(rate * lag.astype(F32))
        turned = rev_ref[n : n + 1, :] * jnp.exp(rate * back.astype(F32))
        rows = slice(n * taps, (n + 1) * taps)
        for source, ref, near in ((turned, fwd_ref, col <= row), (plain, bwd_ref, col >= row)):
            ring = pltpu.roll(jnp.broadcast_to(source, (taps, taps)), 0, 1, stride=1, stride_axis=0)
            ref[rows, :taps] = jnp.where(near, ring, 0.0).astype(BF16)
            ref[rows, taps:] = jnp.where(near, 0.0, ring).astype(BF16)


def project_body(pieces, members, x_ref, own_ref, peer_ref, out_ref):
    rows, width = x_ref.shape
    half = width // 2
    order = row_order(pieces, members, rows // (pieces * members), False)
    x = dot(order, x_ref[...]).astype(BF16)
    streams, _, channels = own_ref.shape
    for i in range(streams):
        part = dot(x[:, :half], own_ref[i]) + dot(x[:, half:], peer_ref[i])
        out_ref[:, :, i * channels : (i + 1) * channels] = part.astype(BF16).reshape(
            members, rows // members, channels
        )


def back_body(pieces, members, g_ref, own_ref, peer_ref, out_ref, turned_ref):
    rows = g_ref.shape[0] * g_ref.shape[1]
    order = row_order(pieces, members, rows // (pieces * members), True)
    streams, half, channels = own_ref.shape
    g = dot(order, g_ref[...].reshape(rows, streams * channels)).astype(BF16)
    turned_ref[...] = g
    for side, ref in ((0, own_ref), (1, peer_ref)):
        total = dot_nt(g[:, :channels], ref[0])
        for i in range(1, streams):
            total = total + dot_nt(g[:, i * channels : (i + 1) * channels], ref[i])
        out_ref[:, side * half : (side + 1) * half] = total.astype(BF16)


def later(x, border, by):
    row = lax.broadcasted_iota(jnp.int32, x.shape, 0)
    moved = pltpu.roll(x, by, 0)
    for i in range(by):
        moved = jnp.where(row == i, border[8 - by + i : 9 - by + i], moved)
    return moved


def sooner(x, border, by):
    count = x.shape[0]
    row = lax.broadcasted_iota(jnp.int32, x.shape, 0)
    moved = pltpu.roll(x, count - by, 0)
    for i in range(by):
        moved = jnp.where(row == count - by + i, border[i : i + 1], moved)
    return moved


def gate_body(tokens, f0_ref, f1_ref, halo_ref, short_ref, up_ref, half_ref, q_ref, k_ref, v_ref, prod_ref, cg_ref):
    count = f0_ref.shape[0] * 2
    order = token_order(half_ref[0, 0], tokens, count, False)
    features = dot(order, jnp.concatenate([f0_ref[...], f1_ref[...]], axis=0))
    channels = up_ref.shape[1]
    outs = (q_ref, k_ref, v_ref)
    halo = halo_ref[...].astype(F32)
    for i in range(3):
        cols = slice(i * channels, (i + 1) * channels)
        x, border = features[:, cols], halo[:, cols]
        total = short_ref[0, i : i + 1] * x
        for lag in range(1, short_ref.shape[0]):
            total = total + short_ref[lag, i : i + 1] * later(x, border, lag)
        outs[i][...] = total
    prod_ref[...] = (k_ref[...] * v_ref[...]).astype(BF16)
    cg_ref[...] = (up_ref[...].astype(F32) * q_ref[...]).astype(BF16)


def convolve(t_ref, own, far):
    both = jnp.concatenate([own, far], axis=0)
    count, channels = own.shape
    filters = t_ref.shape[0] // count
    group = lax.broadcasted_iota(jnp.int32, (1, channels), 1) // (channels // filters)
    total = jnp.zeros((count, channels), F32)
    for n in range(filters):
        part = dot(t_ref[n * count : (n + 1) * count, :], both)
        total = jnp.where(group == n, part, total)
    return total


def hyena_body(fwd_ref, bwd_ref, prod_ref, prev_ref, cg_ref, next_ref, q_ref, k_ref, v_ref, up_ref, skip_ref, out_ref, fg_ref):
    channels = up_ref.shape[1]
    up, q, k, v, skip = up_ref[...].astype(F32), q_ref[...], k_ref[...], v_ref[...], skip_ref[...]
    convolved = convolve(fwd_ref, prod_ref[...], prev_ref[...]) + skip * (k * v)
    out_ref[...] = (q * convolved).astype(BF16)
    fg_ref[:, :channels] = up * convolved
    back = convolve(bwd_ref, cg_ref[...], next_ref[...]) + skip * (up * q)
    fg_ref[:, channels : 2 * channels] = back * v
    fg_ref[:, 2 * channels :] = back * k


def grad_body(tokens, fg_ref, head_ref, short_ref, half_ref, out0_ref, out1_ref):
    count, wide = fg_ref.shape
    channels = wide // 3
    order = token_order(half_ref[0, 0], tokens, count, True)
    for i in range(3):
        cols = slice(i * channels, (i + 1) * channels)
        x, border = fg_ref[:, cols], head_ref[:, cols]
        total = short_ref[0, i : i + 1] * x
        for lag in range(1, short_ref.shape[0]):
            total = total + short_ref[lag, i : i + 1] * sooner(x, border, lag)
        turned = dot(order, total.astype(BF16)).astype(BF16)
        out0_ref[:, cols] = turned[: count // 2]
        out1_ref[:, cols] = turned[count // 2 :]


def swap(x, axis, by=1):
    return lax.ppermute(x, axis, [(i, i ^ by) for i in range(lax.axis_size(axis))])


def shifted(x, by):
    axis = ("zl", "core")
    count = lax.axis_size("zl") * lax.axis_size("core")
    return lax.ppermute(x, axis, [(i, i + by) for i in range(count) if 0 <= i + by < count])


def line_scatter(x):
    count, by = x.shape[0], 1
    while count > 1:
        half = count // 2
        got = swap(x[half:], "zl", by)
        x = (x[:half].astype(F32) + got.astype(F32)).astype(BF16)
        count, by = half, by * 2
    return x[0]


def line_gather(x):
    x = x[None]
    by = lax.axis_size("zl") // 2
    while by:
        x = jnp.concatenate([x, swap(x, "zl", by)], axis=0)
        by //= 2
    return x


def shards(inputs, featurizer, short_filter, long_filter, decay_rate, skip_gain, output_grad):
    tokens, blocks, rows = inputs.shape
    members = lax.axis_size("zl")
    pieces = lax.axis_size("x") * lax.axis_size("y")
    channels = featurizer.shape[2]
    wide = 3 * channels
    count = output_grad.shape[0]
    zl, core, zh = lax.axis_index("zl"), lax.axis_index("core"), lax.axis_index("zh")
    short_filter = short_filter.astype(F32)

    w_own = featurizer.transpose(1, 0, 2)
    w_peer = swap(w_own, "core")
    rolled = jnp.roll(long_filter[:, ::-1], 1, axis=1)
    matrix = shape((long_filter.shape[0] * count, 2 * count), BF16)
    t_fwd, t_bwd = call(toeplitz_body, (matrix, matrix), long_filter, rolled, decay_rate[:, None])

    order = jnp.array(bit_reversed(members), jnp.int32)
    wanted = (((order ^ zl) * 2)[None, :] + (jnp.arange(2, dtype=jnp.int32) ^ core)[:, None]).reshape(-1)
    pick = (wanted[:, None] == jnp.arange(blocks, dtype=jnp.int32)[None, :]).astype(BF16)
    sorted_in = jnp.einsum("kb,tbd->ktd", pick, inputs, preferred_element_type=F32).astype(BF16)
    mine, other = sorted_in[:members], sorted_in[members:]
    local = jnp.concatenate([mine, swap(other, "core")], axis=2).reshape(members * tokens, 2 * rows)

    def spread(x):
        wider = jnp.broadcast_to(x[None], (pieces, *x.shape))
        return lax.all_to_all(wider, ("x", "y"), 0, 0, tiled=True).reshape(-1, x.shape[1])

    far = swap(local, "zh")
    project = functools.partial(project_body, pieces, members)
    part_shape = shape((members, pieces * tokens, wide), BF16)
    x_near = spread(local)
    f_near = line_scatter(call(project, part_shape, x_near, w_own, w_peer))
    x_far = spread(far)
    f_far = line_scatter(call(project, part_shape, x_far, w_own, w_peer))

    last = jnp.where(zh == 1, f_near[-8:], f_far[-8:])
    halo = shifted(last, 1)
    half = zh.astype(jnp.int32).reshape(1, 1)
    upstream = output_grad.reshape(count, channels)
    plane = shape((count, channels), F32)
    thin = shape((count, channels), BF16)
    q, k, v, prod, cg = call(
        functools.partial(gate_body, tokens), (plane, plane, plane, thin, thin), f_near, f_far, halo, short_filter, upstream, half
    )
    prev, nxt = shifted(prod, 1), shifted(cg, -1)
    hyena, fg = call(
        hyena_body,
        (thin, shape((count, wide), F32)),
        t_fwd, t_bwd, prod, prev, cg, nxt, q, k, v, upstream, skip_gain[None, :],
    )
    head = shifted(fg[:8], -1)
    piece_shape = shape((count // 2, wide), BF16)
    g_near, g_far = call(functools.partial(grad_body, tokens), (piece_shape, piece_shape), fg, head, short_filter, half)
    back = functools.partial(back_body, pieces, members)
    back_shapes = (shape((members * pieces * tokens, 2 * rows), BF16), shape((members * pieces * tokens, wide), BF16))

    def collect(x):
        x = lax.all_to_all(x.reshape(pieces, members * tokens, 2 * rows), ("x", "y"), 0, 0, tiled=True)
        return jnp.sum(x.astype(F32), axis=0)

    d_far, turned_far = call(back, back_shapes, line_gather(g_far), w_own, w_peer)
    sent = swap(collect(d_far).astype(BF16), "zh")
    d_near, turned_near = call(back, back_shapes, line_gather(g_near), w_own, w_peer)
    total = (collect(d_near) + sent.astype(F32)).astype(BF16).reshape(members, tokens, 2 * rows)
    both = jnp.concatenate([total[:, :, :rows], swap(total[:, :, rows:], "core")], axis=0)
    input_grad = jnp.einsum("kb,ktd->tbd", pick, both, preferred_element_type=F32).astype(BF16)

    def outer(x, g):
        return lax.dot_general(x, g, (((0,), (0,)), ((), ())), preferred_element_type=F32)

    w_grad = outer(x_near, turned_near) + outer(x_far, turned_far)
    w_far = swap(w_grad[rows:].astype(BF16), "core")
    weight_grad = (w_grad[:rows] + w_far.astype(F32)).astype(BF16).reshape(featurizer.shape)
    return (hyena.reshape(output_grad.shape), input_grad, weight_grad)


def solution(mesh):
    fsdp, tp = (mesh.shape[name] for name in ("fsdp", "tp"))
    side = math.isqrt(tp // 2)
    fine = Mesh(mesh.devices.reshape(fsdp // 2, 2, side, side, 2), ("zl", "core", "x", "y", "zh"))
    f, t = ("zl", "core"), ("x", "y", "zh")
    in_specs = (P(t, None, f), P(f, None, t), P(None, None, t), P(t, None), P(t), P(t), P(None, f, t))
    out_specs = (P(None, f, t), P(t, None, f), P(f, None, t))
    return jax.shard_map(shards, mesh=fine, in_specs=in_specs, out_specs=out_specs, check_vma=False)
```

```python
import functools
import math

import jax
import jax.numpy as jnp
from jax import lax
from jax.experimental import pallas as pl
from jax.experimental.pallas import tpu as pltpu
from jax.sharding import Mesh
from jax.sharding import PartitionSpec as P

F32 = jnp.float32
BF16 = jnp.bfloat16
INTERPRET = False


def call(body, outs, *args, scratch=()):
    whole = pl.BlockSpec(memory_space=pltpu.VMEM)
    scalar = pl.BlockSpec(memory_space=pltpu.SMEM)
    many = isinstance(outs, (tuple, list))
    size = sum(math.prod(a.shape) * a.dtype.itemsize for a in args)
    return pl.pallas_call(
        body,
        out_shape=outs,
        in_specs=[scalar if a.shape == (1,) else whole for a in args],
        out_specs=[whole] * len(outs) if many else whole,
        scratch_shapes=list(scratch),
        cost_estimate=pl.CostEstimate(flops=10**9, bytes_accessed=size, transcendentals=0),
        interpret=INTERPRET,
    )(*args)


def shape(dims, kind):
    return jax.ShapeDtypeStruct(dims, kind)


def dot(a, b):
    return jnp.dot(a, b, preferred_element_type=F32)


def dot_nt(a, b):
    return lax.dot_general(a, b, (((1,), (1,)), ((), ())), preferred_element_type=F32)


def dot_tn(a, b):
    return lax.dot_general(a, b, (((0,), (0,)), ((), ())), preferred_element_type=F32)


def bit_reversed(count):
    bits = count.bit_length() - 1
    return [int(format(i, f"0{bits}b")[::-1], 2) if bits else 0 for i in range(count)]


def row_order(pieces, members, tokens, inverse):
    rows = pieces * members * tokens
    r = lax.broadcasted_iota(jnp.int32, (rows, rows), 0)
    c = lax.broadcasted_iota(jnp.int32, (rows, rows), 1)
    if inverse:
        r, c = c, r
    member, rest = r // (pieces * tokens), r % (pieces * tokens)
    piece, token = rest // tokens, rest % tokens
    return jnp.where(c == (piece * members + member) * tokens + token, 1.0, 0.0).astype(BF16)


def token_order(half, tokens, count, inverse):
    r = lax.broadcasted_iota(jnp.int32, (count, count), 0)
    c = lax.broadcasted_iota(jnp.int32, (count, count), 1)
    if inverse:
        r, c = c, r
    piece, rest = r // (2 * tokens), r % (2 * tokens)
    side, token = rest // tokens, rest % tokens
    relative = jnp.where(side == half, 0, 1)
    return jnp.where(c == relative * (count // 2) + piece * tokens + token, 1.0, 0.0).astype(BF16)


def toeplitz_body(taps_ref, rev_ref, decay_ref, fwd_ref, bwd_ref):
    filters, taps = taps_ref.shape
    lag = lax.broadcasted_iota(jnp.int32, (1, taps), 1)
    back = jnp.where(lag == 0, 0, taps - lag)
    row = lax.broadcasted_iota(jnp.int32, (taps, taps), 0)
    col = lax.broadcasted_iota(jnp.int32, (taps, taps), 1)
    for n in range(filters):
        rate = -decay_ref[n : n + 1, :]
        plain = taps_ref[n : n + 1, :] * jnp.exp(rate * lag.astype(F32))
        turned = rev_ref[n : n + 1, :] * jnp.exp(rate * back.astype(F32))
        rows = slice(n * taps, (n + 1) * taps)
        for source, ref, near in ((turned, fwd_ref, col <= row), (plain, bwd_ref, col >= row)):
            ring = pltpu.roll(jnp.broadcast_to(source, (taps, taps)), 0, 1, stride=1, stride_axis=0)
            ref[rows, :taps] = jnp.where(near, ring, 0.0).astype(BF16)
            ref[rows, taps:] = jnp.where(near, 0.0, ring).astype(BF16)


def project_body(pieces, members, core_ref, x_ref, own_ref, peer_ref, keep_ref, send_ref):
    core = core_ref[0]
    rows = x_ref.shape[1]
    order = row_order(pieces, members, rows // (pieces * members), False)
    mine = dot(order, x_ref[core]).astype(BF16)
    theirs = dot(order, x_ref[1 - core]).astype(BF16)
    streams, _, channels = own_ref.shape
    half = rows // 2
    for i in range(streams):
        cols = slice(i * channels, (i + 1) * channels)
        part = (dot(mine, own_ref[i]) + dot(theirs, peer_ref[i])).astype(BF16)
        keep_ref[:, :, cols] = part[:half].reshape(members // 2, rows // members, channels)
        send_ref[:, :, cols] = part[half:].reshape(members // 2, rows // members, channels)


def back_body(pieces, members, core_ref, g_ref, own_ref, peer_ref, out_ref, turned_ref):
    core = core_ref[0]
    rows = g_ref.shape[0] * g_ref.shape[1]
    order = row_order(pieces, members, rows // (pieces * members), True)
    streams, _, channels = own_ref.shape
    g = dot(order, g_ref[...].reshape(rows, streams * channels)).astype(BF16)
    turned_ref[...] = g
    for place, ref in ((core, own_ref), (1 - core, peer_ref)):
        total = dot_nt(g[:, :channels], ref[0])
        for i in range(1, streams):
            total = total + dot_nt(g[:, i * channels : (i + 1) * channels], ref[i])
        out_ref[place] = total.astype(BF16)


def weight_body(core_ref, x0_ref, x1_ref, g0_ref, g1_ref, own_ref, peer_ref):
    core = core_ref[0]
    streams, _, channels = own_ref.shape
    for place, ref in ((core, own_ref), (1 - core, peer_ref)):
        for i in range(streams):
            cols = slice(i * channels, (i + 1) * channels)
            ref[i] = (dot_tn(x0_ref[place], g0_ref[:, cols]) + dot_tn(x1_ref[place], g1_ref[:, cols])).astype(ref.dtype)


def later(x, border, by):
    row = lax.broadcasted_iota(jnp.int32, x.shape, 0)
    moved = pltpu.roll(x, by, 0)
    for i in range(by):
        moved = jnp.where(row == i, border[8 - by + i : 9 - by + i], moved)
    return moved


def sooner(x, border, by):
    count = x.shape[0]
    row = lax.broadcasted_iota(jnp.int32, x.shape, 0)
    moved = pltpu.roll(x, count - by, 0)
    for i in range(by):
        moved = jnp.where(row == count - by + i, border[i : i + 1], moved)
    return moved


def gate_body(tokens, f0_ref, f1_ref, halo_ref, short_ref, up_ref, half_ref, q_ref, k_ref, v_ref, prod_ref, cg_ref):
    count = f0_ref.shape[0] * 2
    order = token_order(half_ref[0], tokens, count, False)
    features = dot(order, jnp.concatenate([f0_ref[...], f1_ref[...]], axis=0))
    channels = up_ref.shape[1]
    outs = (q_ref, k_ref, v_ref)
    halo = halo_ref[...].astype(F32)
    for i in range(3):
        cols = slice(i * channels, (i + 1) * channels)
        x, border = features[:, cols], halo[:, cols]
        total = short_ref[0, i : i + 1] * x
        for lag in range(1, short_ref.shape[0]):
            total = total + short_ref[lag, i : i + 1] * later(x, border, lag)
        outs[i][...] = total
    prod_ref[...] = (k_ref[...] * v_ref[...]).astype(BF16)
    cg_ref[...] = (up_ref[...].astype(F32) * q_ref[...]).astype(BF16)


def convolve(t_ref, own, far):
    both = jnp.concatenate([own, far], axis=0)
    count, channels = own.shape
    filters = t_ref.shape[0] // count
    group = lax.broadcasted_iota(jnp.int32, (1, channels), 1) // (channels // filters)
    total = jnp.zeros((count, channels), F32)
    for n in range(filters):
        part = dot(t_ref[n * count : (n + 1) * count, :], both)
        total = jnp.where(group == n, part, total)
    return total


def hyena_body(fwd_ref, bwd_ref, prod_ref, prev_ref, cg_ref, next_ref, q_ref, k_ref, v_ref, up_ref, skip_ref, out_ref, fg_ref, head_ref):
    channels = up_ref.shape[1]
    up, q, k, v, skip = up_ref[...].astype(F32), q_ref[...], k_ref[...], v_ref[...], skip_ref[...]
    convolved = convolve(fwd_ref, prod_ref[...], prev_ref[...]) + skip * (k * v)
    out_ref[...] = (q * convolved).astype(BF16)
    fg_ref[:, :channels] = up * convolved
    back = convolve(bwd_ref, cg_ref[...], next_ref[...]) + skip * (up * q)
    fg_ref[:, channels : 2 * channels] = back * v
    fg_ref[:, 2 * channels :] = back * k
    head_ref[...] = fg_ref[:8]


def grad_body(tokens, fg_ref, head_ref, short_ref, half_ref, out0_ref, out1_ref):
    count, wide = fg_ref.shape
    channels = wide // 3
    order = token_order(half_ref[0], tokens, count, True)
    for i in range(3):
        cols = slice(i * channels, (i + 1) * channels)
        x, border = fg_ref[:, cols], head_ref[:, cols]
        total = short_ref[0, i : i + 1] * x
        for lag in range(1, short_ref.shape[0]):
            total = total + short_ref[lag, i : i + 1] * sooner(x, border, lag)
        turned = dot(order, total.astype(BF16)).astype(BF16)
        out0_ref[:, cols] = turned[: count // 2]
        out1_ref[:, cols] = turned[count // 2 :]


def swap(x, axis, by=1):
    return lax.ppermute(x, axis, [(i, i ^ by) for i in range(lax.axis_size(axis))])


def shifted(x, by):
    axis = ("zl", "core")
    count = lax.axis_size("zl") * lax.axis_size("core")
    return lax.ppermute(x, axis, [(i, i + by) for i in range(count) if 0 <= i + by < count])


def line_scatter(keep, send):
    count, by = keep.shape[0], 1
    while True:
        got = swap(send, "zl", by)
        if count == 1:
            return (keep[0].astype(F32) + got[0].astype(F32)).astype(BF16)
        half = count // 2
        send = (keep[half:].astype(F32) + got[half:].astype(F32)).astype(BF16)
        keep = (keep[:half].astype(F32) + got[:half].astype(F32)).astype(BF16)
        count, by = half, by * 2


def line_gather(x, tie=None):
    x = x[None]
    by = lax.axis_size("zl") // 2
    while by:
        if by == 1 and tie is not None:
            x, tie = lax.optimization_barrier((x, tie))
        x = jnp.concatenate([x, swap(x, "zl", by)], axis=0)
        by //= 2
    return x if tie is None else (x, tie)


def shards(inputs, featurizer, short_filter, long_filter, decay_rate, skip_gain, output_grad):
    tokens, blocks, rows = inputs.shape
    members = lax.axis_size("zl")
    pieces = lax.axis_size("x") * lax.axis_size("y")
    lines = members * tokens
    channels = featurizer.shape[2]
    wide = 3 * channels
    count = output_grad.shape[0]
    zl, core, zh = lax.axis_index("zl"), lax.axis_index("core"), lax.axis_index("zh")
    here = core.astype(jnp.int32).reshape(1)
    half = zh.astype(jnp.int32).reshape(1)

    order = jnp.array(bit_reversed(members), jnp.int32) ^ zl
    block = (order[None, :] * 2 + jnp.arange(2, dtype=jnp.int32)[:, None]).reshape(-1, 1)
    source = (jnp.arange(tokens, dtype=jnp.int32)[None, :] * blocks + block).reshape(-1, 1)
    pick = (source == jnp.arange(tokens * blocks, dtype=jnp.int32)[None, :]).astype(BF16)
    local = dot(pick, inputs.reshape(tokens * blocks, rows)).astype(BF16).reshape(2, 1, lines, rows)

    def exchange(x):
        x = lax.all_to_all(x.reshape(2 * pieces, lines, rows), ("core", "x", "y"), 0, 0, tiled=True)
        return x.reshape(2, pieces, lines, rows)

    def spread(x):
        return exchange(jnp.broadcast_to(x, (2, pieces, lines, rows))).reshape(2, pieces * lines, rows)

    x_near = spread(local)
    far = swap(local, "zh")
    w_own = featurizer.transpose(1, 0, 2)
    w_peer = swap(w_own, "core")
    rolled = jnp.roll(long_filter[:, ::-1], 1, axis=1)
    matrix = shape((long_filter.shape[0] * count, 2 * count), BF16)
    t_fwd, t_bwd = call(toeplitz_body, (matrix, matrix), long_filter, rolled, decay_rate[:, None])
    x_near, t_fwd, t_bwd = lax.optimization_barrier((x_near, t_fwd, t_bwd))

    project = functools.partial(project_body, pieces, members)
    part_shape = (shape((members // 2, pieces * tokens, wide), BF16),) * 2
    f_near = line_scatter(*call(project, part_shape, here, x_near, w_own, w_peer))
    x_far = spread(far)
    f_far = line_scatter(*call(project, part_shape, here, x_far, w_own, w_peer))

    last = jnp.where(zh == 1, f_near[-8:], f_far[-8:])
    halo = shifted(last, 1)
    upstream = output_grad.reshape(count, channels)
    plane = shape((count, channels), F32)
    thin = shape((count, channels), BF16)
    q, k, v, prod, cg = call(
        functools.partial(gate_body, tokens), (plane, plane, plane, thin, thin), f_near, f_far, halo, short_filter, upstream, half
    )
    prev, nxt = shifted(prod, 1), shifted(cg, -1)
    hyena, fg, head = call(
        hyena_body,
        (thin, shape((count, wide), F32), shape((8, wide), F32)),
        t_fwd, t_bwd, prod, prev, cg, nxt, q, k, v, upstream, skip_gain[None, :],
    )
    head = shifted(head, -1)
    piece_shape = shape((count // 2, wide), BF16)
    g_near, g_far = call(functools.partial(grad_body, tokens), (piece_shape, piece_shape), fg, head, short_filter, half)
    back = functools.partial(back_body, pieces, members)
    back_shapes = (shape((2, pieces * lines, rows), BF16), shape((pieces * lines, wide), BF16))

    def collect(x):
        return jnp.sum(exchange(x).astype(F32), axis=1)

    d_far, turned_far = call(back, back_shapes, here, line_gather(g_far), w_own, w_peer)
    s_far = collect(d_far).astype(BF16)
    all_near, s_far = line_gather(g_near, s_far)
    sent = swap(s_far, "zh")
    d_near, turned_near = call(back, back_shapes, here, all_near, w_own, w_peer)
    weight_shape = (3, rows, channels)
    w_grad, w_far = call(weight_body, (shape(weight_shape, F32), shape(weight_shape, BF16)), here, x_near, x_far, turned_near, turned_far)
    weight_grad = (w_grad + swap(w_far, "core").astype(F32)).astype(BF16).transpose(1, 0, 2)
    total = (collect(d_near) + sent.astype(F32)).astype(BF16).reshape(2 * lines, rows)
    input_grad = dot_tn(pick, total).astype(BF16).reshape(inputs.shape)
    return (hyena.reshape(output_grad.shape), input_grad, weight_grad)


def solution(mesh):
    fsdp, tp = (mesh.shape[name] for name in ("fsdp", "tp"))
    side = math.isqrt(tp // 2)
    fine = Mesh(mesh.devices.reshape(fsdp // 2, 2, side, side, 2), ("zl", "core", "x", "y", "zh"))
    f, t = ("zl", "core"), ("x", "y", "zh")
    in_specs = (P(t, None, f), P(f, None, t), P(None, None, t), P(t, None), P(t), P(t), P(None, f, t))
    out_specs = (P(None, f, t), P(t, None, f), P(f, None, t))
    return jax.shard_map(shards, mesh=fine, in_specs=in_specs, out_specs=out_specs, check_vma=False)
```

```python
import functools
import math

import jax
import jax.numpy as jnp
from jax import lax
from jax.experimental import pallas as pl
from jax.experimental.pallas import tpu as pltpu
from jax.sharding import Mesh
from jax.sharding import PartitionSpec as P

F32 = jnp.float32
BF16 = jnp.bfloat16
INTERPRET = False


def call(body, outs, *args, scratch=()):
    whole = pl.BlockSpec(memory_space=pltpu.VMEM)
    scalar = pl.BlockSpec(memory_space=pltpu.SMEM)
    many = isinstance(outs, (tuple, list))
    size = sum(math.prod(a.shape) * a.dtype.itemsize for a in args)
    return pl.pallas_call(
        body,
        out_shape=outs,
        in_specs=[scalar if a.shape == (1,) else whole for a in args],
        out_specs=[whole] * len(outs) if many else whole,
        scratch_shapes=list(scratch),
        cost_estimate=pl.CostEstimate(flops=10**9, bytes_accessed=size, transcendentals=0),
        interpret=INTERPRET,
    )(*args)


def shape(dims, kind):
    return jax.ShapeDtypeStruct(dims, kind)


def dot(a, b):
    return jnp.dot(a, b, preferred_element_type=F32)


def dot_nt(a, b):
    return lax.dot_general(a, b, (((1,), (1,)), ((), ())), preferred_element_type=F32)


def dot_tn(a, b):
    return lax.dot_general(a, b, (((0,), (0,)), ((), ())), preferred_element_type=F32)


def bit_reversed(count):
    bits = count.bit_length() - 1
    return [int(format(i, f"0{bits}b")[::-1], 2) if bits else 0 for i in range(count)]


def row_order(pieces, members, tokens, inverse):
    rows = pieces * members * tokens
    r = lax.broadcasted_iota(jnp.int32, (rows, rows), 0)
    c = lax.broadcasted_iota(jnp.int32, (rows, rows), 1)
    if inverse:
        r, c = c, r
    member, rest = r // (pieces * tokens), r % (pieces * tokens)
    piece, token = rest // tokens, rest % tokens
    return jnp.where(c == (piece * members + member) * tokens + token, 1.0, 0.0).astype(BF16)


def token_order(half, tokens, count, inverse):
    r = lax.broadcasted_iota(jnp.int32, (count, count), 0)
    c = lax.broadcasted_iota(jnp.int32, (count, count), 1)
    if inverse:
        r, c = c, r
    piece, rest = r // (2 * tokens), r % (2 * tokens)
    side, token = rest // tokens, rest % tokens
    relative = jnp.where(side == half, 0, 1)
    return jnp.where(c == relative * (count // 2) + piece * tokens + token, 1.0, 0.0).astype(BF16)


def prepare_body(pieces, members, taps_ref, rev_ref, decay_ref, fwd_ref, bwd_ref, turn_ref, unturn_ref):
    tokens = turn_ref.shape[0] // (pieces * members)
    turn_ref[...] = row_order(pieces, members, tokens, False)
    unturn_ref[...] = row_order(pieces, members, tokens, True)
    filters, taps = taps_ref.shape
    lag = lax.broadcasted_iota(jnp.int32, (1, taps), 1)
    back = jnp.where(lag == 0, 0, taps - lag)
    row = lax.broadcasted_iota(jnp.int32, (taps, taps), 0)
    col = lax.broadcasted_iota(jnp.int32, (taps, taps), 1)
    for n in range(filters):
        rate = -decay_ref[n : n + 1, :]
        plain = taps_ref[n : n + 1, :] * jnp.exp(rate * lag.astype(F32))
        turned = rev_ref[n : n + 1, :] * jnp.exp(rate * back.astype(F32))
        rows = slice(n * taps, (n + 1) * taps)
        for source, ref, near in ((turned, fwd_ref, col <= row), (plain, bwd_ref, col >= row)):
            ring = pltpu.roll(jnp.broadcast_to(source, (taps, taps)), 0, 1, stride=1, stride_axis=0)
            ref[rows, :taps] = jnp.where(near, ring, 0.0).astype(BF16)
            ref[rows, taps:] = jnp.where(near, 0.0, ring).astype(BF16)


def project_body(members, core_ref, order_ref, x_ref, own_ref, peer_ref, keep_ref, send_ref):
    core = core_ref[0]
    rows = x_ref.shape[1]
    order = order_ref[...]
    mine = dot(order, x_ref[core]).astype(BF16)
    theirs = dot(order, x_ref[1 - core]).astype(BF16)
    streams, _, channels = own_ref.shape
    half = rows // 2
    for i in range(streams):
        cols = slice(i * channels, (i + 1) * channels)
        part = (dot(mine, own_ref[i]) + dot(theirs, peer_ref[i])).astype(BF16)
        keep_ref[:, :, cols] = part[:half].reshape(members // 2, rows // members, channels)
        send_ref[:, :, cols] = part[half:].reshape(members // 2, rows // members, channels)


def back_body(core_ref, order_ref, *refs):
    *g_refs, own_ref, peer_ref, out_ref, turned_ref = refs
    core = core_ref[0]
    streams, _, channels = own_ref.shape
    gathered = jnp.concatenate([ref[...].reshape(-1, streams * channels) for ref in g_refs], axis=0)
    g = dot(order_ref[...], gathered).astype(BF16)
    turned_ref[...] = g
    for place, ref in ((core, own_ref), (1 - core, peer_ref)):
        total = dot_nt(g[:, :channels], ref[0])
        for i in range(1, streams):
            total = total + dot_nt(g[:, i * channels : (i + 1) * channels], ref[i])
        out_ref[place] = total.astype(BF16)


def weight_body(core_ref, x0_ref, x1_ref, g0_ref, g1_ref, own_ref, peer_ref):
    core = core_ref[0]
    streams, _, channels = own_ref.shape
    for place, ref in ((core, own_ref), (1 - core, peer_ref)):
        for i in range(streams):
            cols = slice(i * channels, (i + 1) * channels)
            ref[i] = (dot_tn(x0_ref[place], g0_ref[:, cols]) + dot_tn(x1_ref[place], g1_ref[:, cols])).astype(ref.dtype)


def later(x, border, by):
    row = lax.broadcasted_iota(jnp.int32, x.shape, 0)
    moved = pltpu.roll(x, by, 0)
    for i in range(by):
        moved = jnp.where(row == i, border[8 - by + i : 9 - by + i], moved)
    return moved


def sooner(x, border, by):
    count = x.shape[0]
    row = lax.broadcasted_iota(jnp.int32, x.shape, 0)
    moved = pltpu.roll(x, count - by, 0)
    for i in range(by):
        moved = jnp.where(row == count - by + i, border[i : i + 1], moved)
    return moved


def gate_body(tokens, f0_ref, f1_ref, halo_ref, short_ref, up_ref, half_ref, q_ref, k_ref, v_ref, prod_ref, cg_ref):
    count = f0_ref.shape[0] * 2
    order = token_order(half_ref[0], tokens, count, False)
    features = dot(order, jnp.concatenate([f0_ref[...], f1_ref[...]], axis=0))
    channels = up_ref.shape[1]
    outs = (q_ref, k_ref, v_ref)
    halo = halo_ref[...].astype(F32)
    for i in range(3):
        cols = slice(i * channels, (i + 1) * channels)
        x, border = features[:, cols], halo[:, cols]
        total = short_ref[0, i : i + 1] * x
        for lag in range(1, short_ref.shape[0]):
            total = total + short_ref[lag, i : i + 1] * later(x, border, lag)
        outs[i][...] = total
    prod_ref[...] = (k_ref[...] * v_ref[...]).astype(BF16)
    cg_ref[...] = (up_ref[...].astype(F32) * q_ref[...]).astype(BF16)


def convolve(t_ref, own, far):
    both = jnp.concatenate([own, far], axis=0)
    count, channels = own.shape
    filters = t_ref.shape[0] // count
    group = lax.broadcasted_iota(jnp.int32, (1, channels), 1) // (channels // filters)
    total = jnp.zeros((count, channels), F32)
    for n in range(filters):
        part = dot(t_ref[n * count : (n + 1) * count, :], both)
        total = jnp.where(group == n, part, total)
    return total


def hyena_body(fwd_ref, bwd_ref, prod_ref, prev_ref, cg_ref, next_ref, q_ref, k_ref, v_ref, up_ref, skip_ref, out_ref, fg_ref, head_ref):
    channels = up_ref.shape[1]
    up, q, k, v, skip = up_ref[...].astype(F32), q_ref[...], k_ref[...], v_ref[...], skip_ref[...]
    convolved = convolve(fwd_ref, prod_ref[...], prev_ref[...]) + skip * (k * v)
    out_ref[...] = (q * convolved).astype(BF16)
    fg_ref[:, :channels] = up * convolved
    back = convolve(bwd_ref, cg_ref[...], next_ref[...]) + skip * (up * q)
    fg_ref[:, channels : 2 * channels] = back * v
    fg_ref[:, 2 * channels :] = back * k
    head_ref[...] = fg_ref[:8]


def grad_body(tokens, fg_ref, head_ref, short_ref, half_ref, out0_ref, out1_ref):
    count, wide = fg_ref.shape
    channels = wide // 3
    order = token_order(half_ref[0], tokens, count, True)
    for i in range(3):
        cols = slice(i * channels, (i + 1) * channels)
        x, border = fg_ref[:, cols], head_ref[:, cols]
        total = short_ref[0, i : i + 1] * x
        for lag in range(1, short_ref.shape[0]):
            total = total + short_ref[lag, i : i + 1] * sooner(x, border, lag)
        turned = dot(order, total.astype(BF16)).astype(BF16)
        out0_ref[:, cols] = turned[: count // 2]
        out1_ref[:, cols] = turned[count // 2 :]


def swap(x, axis, by=1):
    return lax.ppermute(x, axis, [(i, i ^ by) for i in range(lax.axis_size(axis))])


def shifted(x, by):
    axis = ("zl", "core")
    count = lax.axis_size("zl") * lax.axis_size("core")
    return lax.ppermute(x, axis, [(i, i + by) for i in range(count) if 0 <= i + by < count])


def line_scatter(keep, send):
    count, by = keep.shape[0], 1
    while True:
        got = swap(send, "zl", by)
        if count == 1:
            return (keep[0].astype(F32) + got[0].astype(F32)).astype(BF16)
        half = count // 2
        send = (keep[half:].astype(F32) + got[half:].astype(F32)).astype(BF16)
        keep = (keep[:half].astype(F32) + got[:half].astype(F32)).astype(BF16)
        count, by = half, by * 2


def line_gather(x):
    parts = [x[None]]
    by = lax.axis_size("zl") // 2
    while by:
        so_far = jnp.concatenate(parts, axis=0) if len(parts) > 1 else parts[0]
        parts.append(swap(so_far, "zl", by))
        by //= 2
    return parts


def layer(inputs, featurizer, short_filter, long_filter, decay_rate, skip_gain, output_grad):
    tokens, blocks, rows = inputs.shape
    members = lax.axis_size("zl")
    pieces = lax.axis_size("x") * lax.axis_size("y")
    lines = members * tokens
    channels = featurizer.shape[2]
    wide = 3 * channels
    count = output_grad.shape[0]
    zl, core, zh = lax.axis_index("zl"), lax.axis_index("core"), lax.axis_index("zh")
    here = core.astype(jnp.int32).reshape(1)
    half = zh.astype(jnp.int32).reshape(1)

    order = jnp.array(bit_reversed(members), jnp.int32) ^ zl
    block = (order[None, :] * 2 + jnp.arange(2, dtype=jnp.int32)[:, None]).reshape(-1, 1)
    source = (jnp.arange(tokens, dtype=jnp.int32)[None, :] * blocks + block).reshape(-1, 1)
    pick = (source == jnp.arange(tokens * blocks, dtype=jnp.int32)[None, :]).astype(BF16)
    local = dot(pick, inputs.reshape(tokens * blocks, rows)).astype(BF16).reshape(2, 1, lines, rows)

    def exchange(x):
        x = lax.all_to_all(x.reshape(2 * pieces, lines, rows), ("core", "x", "y"), 0, 0, tiled=True)
        return x.reshape(2, pieces, lines, rows)

    def spread(x):
        return exchange(jnp.broadcast_to(x, (2, pieces, lines, rows))).reshape(2, pieces * lines, rows)

    x_near = spread(local)
    far = swap(local, "zh", 1)
    w_own = featurizer.transpose(1, 0, 2)
    w_peer = swap(w_own, "core")
    rolled = jnp.roll(long_filter[:, ::-1], 1, axis=1)
    matrix = shape((long_filter.shape[0] * count, 2 * count), BF16)
    square = shape((pieces * lines, pieces * lines), BF16)
    t_fwd, t_bwd, turn, unturn = call(
        functools.partial(prepare_body, pieces, members),
        (matrix, matrix, square, square),
        long_filter, rolled, decay_rate[:, None],
    )

    project = functools.partial(project_body, members)
    part_shape = (shape((members // 2, pieces * tokens, wide), BF16),) * 2
    parts = call(project, part_shape, here, turn, x_near, w_own, w_peer)
    f_near = line_scatter(*parts)
    x_far = spread(far)
    parts = call(project, part_shape, here, turn, x_far, w_own, w_peer)
    f_far = line_scatter(*parts)

    last = jnp.where(zh == 1, f_near[-8:], f_far[-8:])
    halo = shifted(last, 1)
    upstream = output_grad.reshape(count, channels)
    plane = shape((count, channels), F32)
    thin = shape((count, channels), BF16)
    q, k, v, prod, cg = call(
        functools.partial(gate_body, tokens), (plane, plane, plane, thin, thin), f_near, f_far, halo, short_filter, upstream, half
    )
    prev, nxt = shifted(prod, 1), shifted(cg, -1)
    hyena, fg, head = call(
        hyena_body,
        (thin, shape((count, wide), F32), shape((8, wide), F32)),
        t_fwd, t_bwd, prod, prev, cg, nxt, q, k, v, upstream, skip_gain[None, :],
    )
    head = shifted(head, -1)
    piece_shape = shape((count // 2, wide), BF16)
    g_near, g_far = call(functools.partial(grad_body, tokens), (piece_shape, piece_shape), fg, head, short_filter, half)
    back_shapes = (shape((2, pieces * lines, rows), BF16), shape((pieces * lines, wide), BF16))

    def collect(x):
        x = exchange(x)
        return jnp.sum(x.astype(F32), axis=1)

    d_far, turned_far = call(back_body, back_shapes, here, unturn, *line_gather(g_far), w_own, w_peer)
    sent = swap(collect(d_far).astype(BF16), "zh", 1)
    d_near, turned_near = call(back_body, back_shapes, here, unturn, *line_gather(g_near), w_own, w_peer)
    weight_shape = (3, rows, channels)
    w_grad, w_far = call(weight_body, (shape(weight_shape, F32), shape(weight_shape, BF16)), here, x_near, x_far, turned_near, turned_far)
    weight_grad = (w_grad + swap(w_far, "core").astype(F32)).astype(BF16).transpose(1, 0, 2)
    total = (collect(d_near) + sent.astype(F32)).astype(BF16).reshape(2 * lines, rows)
    input_grad = dot_tn(pick, total).astype(BF16).reshape(inputs.shape)
    return (hyena.reshape(output_grad.shape), input_grad, weight_grad)


def solution(mesh):
    fsdp, tp = (mesh.shape[name] for name in ("fsdp", "tp"))
    side = math.isqrt(tp // 2)
    fine = Mesh(mesh.devices.reshape(fsdp // 2, 2, side, side, 2), ("zl", "core", "x", "y", "zh"))
    f, t = ("zl", "core"), ("x", "y", "zh")
    in_specs = (P(t, None, f), P(f, None, t), P(None, None, t), P(t, None), P(t), P(t), P(None, f, t))
    out_specs = (P(None, f, t), P(t, None, f), P(f, None, t))
    return jax.shard_map(layer, mesh=fine, in_specs=in_specs, out_specs=out_specs, check_vma=False)
```

```python
import functools
import math

import jax
import jax.numpy as jnp
from jax import lax
from jax.experimental import pallas as pl
from jax.experimental.pallas import tpu as pltpu
from jax.sharding import Mesh
from jax.sharding import PartitionSpec as P

F32 = jnp.float32
BF16 = jnp.bfloat16
INTERPRET = False


def call(body, outs, *args, scratch=()):
    whole = pl.BlockSpec(memory_space=pltpu.VMEM)
    scalar = pl.BlockSpec(memory_space=pltpu.SMEM)
    many = isinstance(outs, (tuple, list))
    size = sum(math.prod(a.shape) * a.dtype.itemsize for a in args)
    return pl.pallas_call(
        body,
        out_shape=outs,
        in_specs=[scalar if a.shape == (1,) else whole for a in args],
        out_specs=[whole] * len(outs) if many else whole,
        scratch_shapes=list(scratch),
        cost_estimate=pl.CostEstimate(flops=10**9, bytes_accessed=size, transcendentals=0),
        interpret=INTERPRET,
    )(*args)


def shape(dims, kind):
    return jax.ShapeDtypeStruct(dims, kind)


def dot(a, b):
    return jnp.dot(a, b, preferred_element_type=F32)


def dot_nt(a, b):
    return lax.dot_general(a, b, (((1,), (1,)), ((), ())), preferred_element_type=F32)


def dot_tn(a, b):
    return lax.dot_general(a, b, (((0,), (0,)), ((), ())), preferred_element_type=F32)


def bit_reversed(count):
    bits = count.bit_length() - 1
    return [int(format(i, f"0{bits}b")[::-1], 2) if bits else 0 for i in range(count)]


def row_order(pieces, members, tokens, inverse):
    rows = pieces * members * tokens
    r = lax.broadcasted_iota(jnp.int32, (rows, rows), 0)
    c = lax.broadcasted_iota(jnp.int32, (rows, rows), 1)
    if inverse:
        r, c = c, r
    member, rest = r // (pieces * tokens), r % (pieces * tokens)
    piece, token = rest // tokens, rest % tokens
    return jnp.where(c == (piece * members + member) * tokens + token, 1.0, 0.0).astype(BF16)


def token_order(half, tokens, count, inverse):
    r = lax.broadcasted_iota(jnp.int32, (count, count), 0)
    c = lax.broadcasted_iota(jnp.int32, (count, count), 1)
    if inverse:
        r, c = c, r
    piece, rest = r // (2 * tokens), r % (2 * tokens)
    side, token = rest // tokens, rest % tokens
    relative = jnp.where(side == half, 0, 1)
    return jnp.where(c == relative * (count // 2) + piece * tokens + token, 1.0, 0.0).astype(BF16)


def prepare_body(pieces, members, taps_ref, rev_ref, decay_ref, fwd_ref, bwd_ref, turn_ref, unturn_ref):
    tokens = turn_ref.shape[0] // (pieces * members)
    turn_ref[...] = row_order(pieces, members, tokens, False)
    unturn_ref[...] = row_order(pieces, members, tokens, True)
    filters, taps = taps_ref.shape
    lag = lax.broadcasted_iota(jnp.int32, (1, taps), 1)
    back = jnp.where(lag == 0, 0, taps - lag)
    row = lax.broadcasted_iota(jnp.int32, (taps, taps), 0)
    col = lax.broadcasted_iota(jnp.int32, (taps, taps), 1)
    for n in range(filters):
        rate = -decay_ref[n : n + 1, :]
        plain = taps_ref[n : n + 1, :] * jnp.exp(rate * lag.astype(F32))
        turned = rev_ref[n : n + 1, :] * jnp.exp(rate * back.astype(F32))
        rows = slice(n * taps, (n + 1) * taps)
        for source, ref, near in ((turned, fwd_ref, col <= row), (plain, bwd_ref, col >= row)):
            ring = pltpu.roll(jnp.broadcast_to(source, (taps, taps)), 0, 1, stride=1, stride_axis=0)
            ref[rows, :taps] = jnp.where(near, ring, 0.0).astype(BF16)
            ref[rows, taps:] = jnp.where(near, 0.0, ring).astype(BF16)


def project_body(members, core_ref, order_ref, x_ref, own_ref, peer_ref, keep_ref, send_ref):
    core = core_ref[0]
    rows = x_ref.shape[1]
    order = order_ref[...]
    mine = dot(order, x_ref[core]).astype(BF16)
    theirs = dot(order, x_ref[1 - core]).astype(BF16)
    streams, _, channels = own_ref.shape
    half = rows // 2
    for i in range(streams):
        cols = slice(i * channels, (i + 1) * channels)
        part = (dot(mine, own_ref[i]) + dot(theirs, peer_ref[i])).astype(BF16)
        keep_ref[:, :, cols] = part[:half].reshape(members // 2, rows // members, channels)
        send_ref[:, :, cols] = part[half:].reshape(members // 2, rows // members, channels)


def back_body(core_ref, order_ref, *refs):
    *g_refs, own_ref, peer_ref, out_ref, turned_ref = refs
    core = core_ref[0]
    streams, _, channels = own_ref.shape
    gathered = jnp.concatenate([ref[...].reshape(-1, streams * channels) for ref in g_refs], axis=0)
    g = dot(order_ref[...], gathered).astype(BF16)
    turned_ref[...] = g
    for place, ref in ((core, own_ref), (1 - core, peer_ref)):
        total = dot_nt(g[:, :channels], ref[0])
        for i in range(1, streams):
            total = total + dot_nt(g[:, i * channels : (i + 1) * channels], ref[i])
        out_ref[place] = total.astype(BF16)


def weight_body(core_ref, x0_ref, x1_ref, g0_ref, g1_ref, own_ref, peer_ref):
    core = core_ref[0]
    streams, _, channels = own_ref.shape
    for place, ref in ((core, own_ref), (1 - core, peer_ref)):
        for i in range(streams):
            cols = slice(i * channels, (i + 1) * channels)
            ref[i] = (dot_tn(x0_ref[place], g0_ref[:, cols]) + dot_tn(x1_ref[place], g1_ref[:, cols])).astype(ref.dtype)


def later(x, border, by):
    row = lax.broadcasted_iota(jnp.int32, x.shape, 0)
    moved = pltpu.roll(x, by, 0)
    for i in range(by):
        moved = jnp.where(row == i, border[8 - by + i : 9 - by + i], moved)
    return moved


def sooner(x, border, by):
    count = x.shape[0]
    row = lax.broadcasted_iota(jnp.int32, x.shape, 0)
    moved = pltpu.roll(x, count - by, 0)
    for i in range(by):
        moved = jnp.where(row == count - by + i, border[i : i + 1], moved)
    return moved


def gate_body(tokens, f0_ref, f1_ref, tail_ref, head_ref, short_ref, up_ref, after_ref, half_ref, q_ref, k_ref, v_ref, n_ref, prod_ref, cg_ref):
    count = f0_ref.shape[0] * 2
    order = token_order(half_ref[0], tokens, count, False)
    features = dot(order, jnp.concatenate([f0_ref[...], f1_ref[...]], axis=0))
    channels = up_ref.shape[1]
    outs = (q_ref, k_ref, v_ref)
    tail = tail_ref[...].astype(F32)
    head = head_ref[...].astype(F32)
    for i in range(3):
        cols = slice(i * channels, (i + 1) * channels)
        own, border = features[:, cols], tail[:, cols]
        following, own_tail = head[:, cols], features[count - 8 :, cols]
        total = short_ref[0, i : i + 1] * own
        ahead = short_ref[0, i : i + 1] * following
        for lag in range(1, short_ref.shape[0]):
            total = total + short_ref[lag, i : i + 1] * later(own, border, lag)
            ahead = ahead + short_ref[lag, i : i + 1] * later(following, own_tail, lag)
        outs[i][...] = total
        n_ref[i] = ahead
    prod_ref[...] = (k_ref[...] * v_ref[...]).astype(BF16)
    cg_ref[:count] = (up_ref[...].astype(F32) * q_ref[...]).astype(BF16)
    first = after_ref[...].astype(F32) * n_ref[0]
    row = lax.broadcasted_iota(jnp.int32, first.shape, 0)
    cg_ref[count:] = jnp.where(row == 0, first, 0.0).astype(BF16)


def convolve(t_ref, both, rows):
    count, channels = both.shape[0] // 2, both.shape[1]
    filters = t_ref.shape[0] // count
    group = lax.broadcasted_iota(jnp.int32, (1, channels), 1) // (channels // filters)
    total = jnp.zeros((rows, channels), F32)
    for n in range(filters):
        part = dot(t_ref[n * count : n * count + rows, :], both)
        total = jnp.where(group == n, part, total)
    return total


def hyena_body(
    tokens, fwd_ref, bwd_ref, prod_ref, prev_ref, cg_ref, next_ref, q_ref, k_ref, v_ref, n_ref, up_ref, after_ref, skip_ref, short_ref, half_ref,
    out_ref, g0_ref, g1_ref,
):
    count, channels = up_ref.shape
    ahead = after_ref.shape[0]
    up, q, k, v, skip = up_ref[...].astype(F32), q_ref[...], k_ref[...], v_ref[...], skip_ref[...]
    convolved = convolve(fwd_ref, jnp.concatenate([prod_ref[...], prev_ref[...]], axis=0), count) + skip * (k * v)
    out_ref[...] = (q * convolved).astype(BF16)
    following = next_ref[...]
    back = convolve(bwd_ref, jnp.concatenate([cg_ref[:count], following[:count]], axis=0), count) + skip * (up * q)
    up_n, q_n, k_n, v_n = after_ref[...].astype(F32), n_ref[0], n_ref[1], n_ref[2]
    pad = jnp.zeros((count - ahead, channels), BF16)
    both = jnp.concatenate([(k_n * v_n).astype(BF16), pad, prod_ref[...]], axis=0)
    convolved_n = convolve(fwd_ref, both, ahead) + skip * (k_n * v_n)
    back_n = convolve(bwd_ref, jnp.concatenate([following, pad], axis=0), ahead) + skip * (up_n * q_n)
    order = token_order(half_ref[0], tokens, count, True)
    grads = ((up * convolved, up_n * convolved_n), (back * v, back_n * v_n), (back * k, back_n * k_n))
    for i, (x, border) in enumerate(grads):
        cols = slice(i * channels, (i + 1) * channels)
        total = short_ref[0, i : i + 1] * x
        for lag in range(1, short_ref.shape[0]):
            total = total + short_ref[lag, i : i + 1] * sooner(x, border, lag)
        turned = dot(order, total.astype(BF16)).astype(BF16)
        g0_ref[:, cols] = turned[: count // 2]
        g1_ref[:, cols] = turned[count // 2 :]


def swap(x, axis, by=1):
    return lax.ppermute(x, axis, [(i, i ^ by) for i in range(lax.axis_size(axis))])


def shifted(x, by):
    axis = ("zl", "core")
    count = lax.axis_size("zl") * lax.axis_size("core")
    return lax.ppermute(x, axis, [(i, i + by) for i in range(count) if 0 <= i + by < count])


def line_scatter(keep, send):
    count, by = keep.shape[0], 1
    while True:
        got = swap(send, "zl", by)
        if count == 1:
            return (keep[0].astype(F32) + got[0].astype(F32)).astype(BF16)
        half = count // 2
        send = (keep[half:].astype(F32) + got[half:].astype(F32)).astype(BF16)
        keep = (keep[:half].astype(F32) + got[:half].astype(F32)).astype(BF16)
        count, by = half, by * 2


def line_gather(x):
    parts = [x[None]]
    by = lax.axis_size("zl") // 2
    while by:
        so_far = jnp.concatenate(parts, axis=0) if len(parts) > 1 else parts[0]
        parts.append(swap(so_far, "zl", by))
        by //= 2
    return parts


def layer(inputs, featurizer, short_filter, long_filter, decay_rate, skip_gain, output_grad):
    tokens, blocks, rows = inputs.shape
    members = lax.axis_size("zl")
    pieces = lax.axis_size("x") * lax.axis_size("y")
    lines = members * tokens
    channels = featurizer.shape[2]
    wide = 3 * channels
    count = output_grad.shape[0]
    zl, core, zh = lax.axis_index("zl"), lax.axis_index("core"), lax.axis_index("zh")
    here = core.astype(jnp.int32).reshape(1)
    half = zh.astype(jnp.int32).reshape(1)

    order = jnp.array(bit_reversed(members), jnp.int32) ^ zl
    block = (order[None, :] * 2 + jnp.arange(2, dtype=jnp.int32)[:, None]).reshape(-1, 1)
    source = (jnp.arange(tokens, dtype=jnp.int32)[None, :] * blocks + block).reshape(-1, 1)
    pick = (source == jnp.arange(tokens * blocks, dtype=jnp.int32)[None, :]).astype(BF16)
    local = dot(pick, inputs.reshape(tokens * blocks, rows)).astype(BF16).reshape(2, 1, lines, rows)

    def exchange(x):
        x = lax.all_to_all(x.reshape(2 * pieces, lines, rows), ("core", "x", "y"), 0, 0, tiled=True)
        return x.reshape(2, pieces, lines, rows)

    def spread(x):
        return exchange(jnp.broadcast_to(x, (2, pieces, lines, rows))).reshape(2, pieces * lines, rows)

    x_near = spread(local)
    upstream = output_grad.reshape(count, channels)
    after = shifted(upstream[:16], -1)
    far = swap(local, "zh", 1)
    w_own = featurizer.transpose(1, 0, 2)
    w_peer = swap(w_own, "core")
    rolled = jnp.roll(long_filter[:, ::-1], 1, axis=1)
    matrix = shape((long_filter.shape[0] * count, 2 * count), BF16)
    square = shape((pieces * lines, pieces * lines), BF16)
    t_fwd, t_bwd, turn, unturn = call(
        functools.partial(prepare_body, pieces, members),
        (matrix, matrix, square, square),
        long_filter, rolled, decay_rate[:, None],
    )

    project = functools.partial(project_body, members)
    part_shape = (shape((members // 2, pieces * tokens, wide), BF16),) * 2
    parts = call(project, part_shape, here, turn, x_near, w_own, w_peer)
    f_near = line_scatter(*parts)
    x_far = spread(far)
    parts = call(project, part_shape, here, turn, x_far, w_own, w_peer)
    f_far = line_scatter(*parts)

    tail = shifted(jnp.where(zh == 1, f_near[-8:], f_far[-8:]), 1)
    head = shifted(jnp.where(zh == 0, f_near[:16], f_far[:16]), -1)
    plane = shape((count, channels), F32)
    thin = shape((count, channels), BF16)
    longer = shape((count + 16, channels), BF16)
    q, k, v, ahead, prod, cg = call(
        functools.partial(gate_body, tokens),
        (plane, plane, plane, shape((3, 16, channels), F32), thin, longer),
        f_near, f_far, tail, head, short_filter, upstream, after, half,
    )
    prev, nxt = shifted(prod, 1), shifted(cg, -1)
    piece_shape = shape((count // 2, wide), BF16)
    hyena, g_near, g_far = call(
        functools.partial(hyena_body, tokens),
        (thin, piece_shape, piece_shape),
        t_fwd, t_bwd, prod, prev, cg, nxt, q, k, v, ahead, upstream, after, skip_gain[None, :], short_filter, half,
    )
    back_shapes = (shape((2, pieces * lines, rows), BF16), shape((pieces * lines, wide), BF16))

    def collect(x):
        x = exchange(x)
        return jnp.sum(x.astype(F32), axis=1)

    d_far, turned_far = call(back_body, back_shapes, here, unturn, *line_gather(g_far), w_own, w_peer)
    sent = swap(collect(d_far).astype(BF16), "zh", 1)
    d_near, turned_near = call(back_body, back_shapes, here, unturn, *line_gather(g_near), w_own, w_peer)
    weight_shape = (3, rows, channels)
    w_grad, w_far = call(weight_body, (shape(weight_shape, F32), shape(weight_shape, BF16)), here, x_near, x_far, turned_near, turned_far)
    weight_grad = (w_grad + swap(w_far, "core").astype(F32)).astype(BF16).transpose(1, 0, 2)
    total = (collect(d_near) + sent.astype(F32)).astype(BF16).reshape(2 * lines, rows)
    input_grad = dot_tn(pick, total).astype(BF16).reshape(inputs.shape)
    return (hyena.reshape(output_grad.shape), input_grad, weight_grad)


def solution(mesh):
    fsdp, tp = (mesh.shape[name] for name in ("fsdp", "tp"))
    side = math.isqrt(tp // 2)
    fine = Mesh(mesh.devices.reshape(fsdp // 2, 2, side, side, 2), ("zl", "core", "x", "y", "zh"))
    f, t = ("zl", "core"), ("x", "y", "zh")
    in_specs = (P(t, None, f), P(f, None, t), P(None, None, t), P(t, None), P(t), P(t), P(None, f, t))
    out_specs = (P(None, f, t), P(t, None, f), P(f, None, t))
    return jax.shard_map(layer, mesh=fine, in_specs=in_specs, out_specs=out_specs, check_vma=False)
```

```python
import functools
import math

import jax
import jax.numpy as jnp
from jax import lax
from jax.experimental import pallas as pl
from jax.experimental.pallas import tpu as pltpu
from jax.sharding import Mesh
from jax.sharding import PartitionSpec as P

F32 = jnp.float32
BF16 = jnp.bfloat16
INTERPRET = False


def call(body, outs, *args, scratch=()):
    whole = pl.BlockSpec(memory_space=pltpu.VMEM)
    scalar = pl.BlockSpec(memory_space=pltpu.SMEM)
    many = isinstance(outs, (tuple, list))
    size = sum(math.prod(a.shape) * a.dtype.itemsize for a in args)
    return pl.pallas_call(
        body,
        out_shape=outs,
        in_specs=[scalar if a.shape == (1,) else whole for a in args],
        out_specs=[whole] * len(outs) if many else whole,
        scratch_shapes=list(scratch),
        cost_estimate=pl.CostEstimate(flops=10**9, bytes_accessed=size, transcendentals=0),
        interpret=INTERPRET,
    )(*args)


def shape(dims, kind):
    return jax.ShapeDtypeStruct(dims, kind)


def dot(a, b):
    return jnp.dot(a, b, preferred_element_type=F32)


def dot_nt(a, b):
    return lax.dot_general(a, b, (((1,), (1,)), ((), ())), preferred_element_type=F32)


def dot_tn(a, b):
    return lax.dot_general(a, b, (((0,), (0,)), ((), ())), preferred_element_type=F32)


def bit_reversed(count):
    bits = count.bit_length() - 1
    return [int(format(i, f"0{bits}b")[::-1], 2) if bits else 0 for i in range(count)]


def row_order(pieces, members, tokens, inverse):
    rows = pieces * members * tokens
    r = lax.broadcasted_iota(jnp.int32, (rows, rows), 0)
    c = lax.broadcasted_iota(jnp.int32, (rows, rows), 1)
    if inverse:
        r, c = c, r
    member, rest = r // (pieces * tokens), r % (pieces * tokens)
    piece, token = rest // tokens, rest % tokens
    return jnp.where(c == (piece * members + member) * tokens + token, 1.0, 0.0).astype(BF16)


def token_order(half, tokens, count, inverse):
    r = lax.broadcasted_iota(jnp.int32, (count, count), 0)
    c = lax.broadcasted_iota(jnp.int32, (count, count), 1)
    if inverse:
        r, c = c, r
    piece, rest = r // (2 * tokens), r % (2 * tokens)
    side, token = rest // tokens, rest % tokens
    relative = jnp.where(side == half, 0, 1)
    return jnp.where(c == relative * (count // 2) + piece * tokens + token, 1.0, 0.0).astype(BF16)


def prepare_body(pieces, members, taps_ref, rev_ref, decay_ref, fwd_ref, bwd_ref, keep_ref, send_ref, unturn_ref):
    rows = unturn_ref.shape[0]
    tokens = rows // (pieces * members)
    turn = row_order(pieces, members, tokens, False)
    keep_ref[...] = turn[: rows // 2]
    send_ref[...] = turn[rows // 2 :]
    unturn_ref[...] = row_order(pieces, members, tokens, True)
    filters, taps = taps_ref.shape
    lag = lax.broadcasted_iota(jnp.int32, (1, taps), 1)
    back = jnp.where(lag == 0, 0, taps - lag)
    row = lax.broadcasted_iota(jnp.int32, (taps, taps), 0)
    col = lax.broadcasted_iota(jnp.int32, (taps, taps), 1)
    for n in range(filters):
        rate = -decay_ref[n : n + 1, :]
        plain = taps_ref[n : n + 1, :] * jnp.exp(rate * lag.astype(F32))
        turned = rev_ref[n : n + 1, :] * jnp.exp(rate * back.astype(F32))
        rows = slice(n * taps, (n + 1) * taps)
        for source, ref, near in ((turned, fwd_ref, col <= row), (plain, bwd_ref, col >= row)):
            ring = pltpu.roll(jnp.broadcast_to(source, (taps, taps)), 0, 1, stride=1, stride_axis=0)
            ref[rows, :taps] = jnp.where(near, ring, 0.0).astype(BF16)
            ref[rows, taps:] = jnp.where(near, 0.0, ring).astype(BF16)


def project_body(core_ref, order_ref, x_ref, own_ref, peer_ref, out_ref):
    core = core_ref[0]
    members, rows, _ = out_ref.shape
    order = order_ref[...]
    mine = dot(order, x_ref[core]).astype(BF16)
    theirs = dot(order, x_ref[1 - core]).astype(BF16)
    streams, _, channels = own_ref.shape
    for i in range(streams):
        part = (dot(mine, own_ref[i]) + dot(theirs, peer_ref[i])).astype(BF16)
        out_ref[:, :, i * channels : (i + 1) * channels] = part.reshape(members, rows, channels)


def back_body(core_ref, order_ref, *refs):
    *g_refs, own_ref, peer_ref, out_ref, turned_ref = refs
    core = core_ref[0]
    streams, _, channels = own_ref.shape
    gathered = jnp.concatenate([ref[...].reshape(-1, streams * channels) for ref in g_refs], axis=0)
    g = dot(order_ref[...], gathered).astype(BF16)
    turned_ref[...] = g
    for place, ref in ((core, own_ref), (1 - core, peer_ref)):
        total = dot_nt(g[:, :channels], ref[0])
        for i in range(1, streams):
            total = total + dot_nt(g[:, i * channels : (i + 1) * channels], ref[i])
        out_ref[place] = total.astype(BF16)


def weight_body(core_ref, x0_ref, x1_ref, g0_ref, g1_ref, own_ref, peer_ref):
    core = core_ref[0]
    streams, _, channels = own_ref.shape
    for place, ref in ((core, own_ref), (1 - core, peer_ref)):
        for i in range(streams):
            cols = slice(i * channels, (i + 1) * channels)
            ref[i] = (dot_tn(x0_ref[place], g0_ref[:, cols]) + dot_tn(x1_ref[place], g1_ref[:, cols])).astype(ref.dtype)


def later(x, border, by):
    row = lax.broadcasted_iota(jnp.int32, x.shape, 0)
    moved = pltpu.roll(x, by, 0)
    for i in range(by):
        moved = jnp.where(row == i, border[8 - by + i : 9 - by + i], moved)
    return moved


def sooner(x, border, by):
    count = x.shape[0]
    row = lax.broadcasted_iota(jnp.int32, x.shape, 0)
    moved = pltpu.roll(x, count - by, 0)
    for i in range(by):
        moved = jnp.where(row == count - by + i, border[i : i + 1], moved)
    return moved


def gate_body(tokens, f0_ref, f1_ref, tail_ref, head_ref, short_ref, up_ref, after_ref, half_ref, q_ref, k_ref, v_ref, n_ref, prod_ref, cg_ref):
    count = f0_ref.shape[0] * 2
    order = token_order(half_ref[0], tokens, count, False)
    features = dot(order, jnp.concatenate([f0_ref[...], f1_ref[...]], axis=0))
    channels = up_ref.shape[1]
    outs = (q_ref, k_ref, v_ref)
    tail = tail_ref[...].astype(F32)
    head = head_ref[...].astype(F32)
    for i in range(3):
        cols = slice(i * channels, (i + 1) * channels)
        own, border = features[:, cols], tail[:, cols]
        following, own_tail = head[:, cols], features[count - 8 :, cols]
        total = short_ref[0, i : i + 1] * own
        ahead = short_ref[0, i : i + 1] * following
        for lag in range(1, short_ref.shape[0]):
            total = total + short_ref[lag, i : i + 1] * later(own, border, lag)
            ahead = ahead + short_ref[lag, i : i + 1] * later(following, own_tail, lag)
        outs[i][...] = total
        n_ref[i] = ahead
    prod_ref[...] = (k_ref[...] * v_ref[...]).astype(BF16)
    cg_ref[:count] = (up_ref[...].astype(F32) * q_ref[...]).astype(BF16)
    first = after_ref[...].astype(F32) * n_ref[0]
    row = lax.broadcasted_iota(jnp.int32, first.shape, 0)
    cg_ref[count:] = jnp.where(row == 0, first, 0.0).astype(BF16)


def convolve(t_ref, both, rows):
    count, channels = both.shape[0] // 2, both.shape[1]
    filters = t_ref.shape[0] // count
    group = lax.broadcasted_iota(jnp.int32, (1, channels), 1) // (channels // filters)
    total = jnp.zeros((rows, channels), F32)
    for n in range(filters):
        part = dot(t_ref[n * count : n * count + rows, :], both)
        total = jnp.where(group == n, part, total)
    return total


def hyena_body(
    tokens, fwd_ref, bwd_ref, prod_ref, prev_ref, cg_ref, next_ref, q_ref, k_ref, v_ref, n_ref, up_ref, after_ref, skip_ref, short_ref, half_ref,
    out_ref, g0_ref, g1_ref,
):
    count, channels = up_ref.shape
    ahead = after_ref.shape[0]
    up, q, k, v, skip = up_ref[...].astype(F32), q_ref[...], k_ref[...], v_ref[...], skip_ref[...]
    convolved = convolve(fwd_ref, jnp.concatenate([prod_ref[...], prev_ref[...]], axis=0), count) + skip * (k * v)
    out_ref[...] = (q * convolved).astype(BF16)
    following = next_ref[...]
    back = convolve(bwd_ref, jnp.concatenate([cg_ref[:count], following[:count]], axis=0), count) + skip * (up * q)
    up_n, q_n, k_n, v_n = after_ref[...].astype(F32), n_ref[0], n_ref[1], n_ref[2]
    pad = jnp.zeros((count - ahead, channels), BF16)
    both = jnp.concatenate([(k_n * v_n).astype(BF16), pad, prod_ref[...]], axis=0)
    convolved_n = convolve(fwd_ref, both, ahead) + skip * (k_n * v_n)
    back_n = convolve(bwd_ref, jnp.concatenate([following, pad], axis=0), ahead) + skip * (up_n * q_n)
    order = token_order(half_ref[0], tokens, count, True)
    grads = ((up * convolved, up_n * convolved_n), (back * v, back_n * v_n), (back * k, back_n * k_n))
    for i, (x, border) in enumerate(grads):
        cols = slice(i * channels, (i + 1) * channels)
        total = short_ref[0, i : i + 1] * x
        for lag in range(1, short_ref.shape[0]):
            total = total + short_ref[lag, i : i + 1] * sooner(x, border, lag)
        turned = dot(order, total.astype(BF16)).astype(BF16)
        g0_ref[:, cols] = turned[: count // 2]
        g1_ref[:, cols] = turned[count // 2 :]


def swap(x, axis, by=1):
    return lax.ppermute(x, axis, [(i, i ^ by) for i in range(lax.axis_size(axis))])


def shifted(x, by):
    axis = ("zl", "core")
    count = lax.axis_size("zl") * lax.axis_size("core")
    return lax.ppermute(x, axis, [(i, i + by) for i in range(count) if 0 <= i + by < count])


def line_scatter(keep, send):
    count, by = keep.shape[0], 1
    while True:
        got = swap(send, "zl", by)
        if count == 1:
            return (keep[0].astype(F32) + got[0].astype(F32)).astype(BF16)
        half = count // 2
        send = (keep[half:].astype(F32) + got[half:].astype(F32)).astype(BF16)
        keep = (keep[:half].astype(F32) + got[:half].astype(F32)).astype(BF16)
        count, by = half, by * 2


def line_gather(x):
    parts = [x[None]]
    by = lax.axis_size("zl") // 2
    while by:
        so_far = jnp.concatenate(parts, axis=0) if len(parts) > 1 else parts[0]
        parts.append(swap(so_far, "zl", by))
        by //= 2
    return parts


def layer(inputs, featurizer, short_filter, long_filter, decay_rate, skip_gain, output_grad):
    tokens, blocks, rows = inputs.shape
    members = lax.axis_size("zl")
    pieces = lax.axis_size("x") * lax.axis_size("y")
    lines = members * tokens
    channels = featurizer.shape[2]
    wide = 3 * channels
    count = output_grad.shape[0]
    zl, core, zh = lax.axis_index("zl"), lax.axis_index("core"), lax.axis_index("zh")
    here = core.astype(jnp.int32).reshape(1)
    half = zh.astype(jnp.int32).reshape(1)

    order = jnp.array(bit_reversed(members), jnp.int32) ^ zl
    block = (order[None, :] * 2 + jnp.arange(2, dtype=jnp.int32)[:, None]).reshape(-1, 1)
    source = (jnp.arange(tokens, dtype=jnp.int32)[None, :] * blocks + block).reshape(-1, 1)
    pick = (source == jnp.arange(tokens * blocks, dtype=jnp.int32)[None, :]).astype(BF16)
    local = dot(pick, inputs.reshape(tokens * blocks, rows)).astype(BF16).reshape(2, 1, lines, rows)

    def exchange(x):
        x = lax.all_to_all(x.reshape(2 * pieces, lines, rows), ("core", "x", "y"), 0, 0, tiled=True)
        return x.reshape(2, pieces, lines, rows)

    def spread(x):
        return exchange(jnp.broadcast_to(x, (2, pieces, lines, rows))).reshape(2, pieces * lines, rows)

    x_near = spread(local)
    upstream = output_grad.reshape(count, channels)
    after = shifted(upstream[:16], -1)
    far = swap(local, "zh", 1)
    w_own = featurizer.transpose(1, 0, 2)
    w_peer = swap(w_own, "core", 1)
    rolled = jnp.roll(long_filter[:, ::-1], 1, axis=1)
    matrix = shape((long_filter.shape[0] * count, 2 * count), BF16)
    oblong = shape((pieces * lines // 2, pieces * lines), BF16)
    square = shape((pieces * lines, pieces * lines), BF16)
    t_fwd, t_bwd, turn_keep, turn_send, unturn = call(
        functools.partial(prepare_body, pieces, members),
        (matrix, matrix, oblong, oblong, square),
        long_filter, rolled, decay_rate[:, None],
    )

    part_shape = shape((members // 2, pieces * tokens, wide), BF16)

    def project(x):
        send = call(project_body, part_shape, here, turn_send, x, w_own, w_peer)
        keep = call(project_body, part_shape, here, turn_keep, x, w_own, w_peer)
        return line_scatter(keep, send)

    f_near = project(x_near)
    x_far = spread(far)
    f_far = project(x_far)
    tail = shifted(jnp.where(zh == 1, f_near[-8:], f_far[-8:]), 1)
    head = shifted(jnp.where(zh == 0, f_near[:16], f_far[:16]), -1)
    plane = shape((count, channels), F32)
    thin = shape((count, channels), BF16)
    longer = shape((count + 16, channels), BF16)
    q, k, v, ahead, prod, cg = call(
        functools.partial(gate_body, tokens),
        (plane, plane, plane, shape((3, 16, channels), F32), thin, longer),
        f_near, f_far, tail, head, short_filter, upstream, after, half,
    )
    prev, nxt = shifted(prod, 1), shifted(cg, -1)
    piece_shape = shape((count // 2, wide), BF16)
    hyena, g_near, g_far = call(
        functools.partial(hyena_body, tokens),
        (thin, piece_shape, piece_shape),
        t_fwd, t_bwd, prod, prev, cg, nxt, q, k, v, ahead, upstream, after, skip_gain[None, :], short_filter, half,
    )
    back_shapes = (shape((2, pieces * lines, rows), BF16), shape((pieces * lines, wide), BF16))

    def collect(x):
        x = exchange(x)
        return jnp.sum(x.astype(F32), axis=1)

    d_far, turned_far = call(back_body, back_shapes, here, unturn, *line_gather(g_far), w_own, w_peer)
    sent = swap(collect(d_far).astype(BF16), "zh", 1)
    d_near, turned_near = call(back_body, back_shapes, here, unturn, *line_gather(g_near), w_own, w_peer)
    weight_shape = (3, rows, channels)
    w_grad, w_far = call(weight_body, (shape(weight_shape, F32), shape(weight_shape, BF16)), here, x_near, x_far, turned_near, turned_far)
    weight_grad = (w_grad + swap(w_far, "core").astype(F32)).astype(BF16).transpose(1, 0, 2)
    total = (collect(d_near) + sent.astype(F32)).astype(BF16).reshape(2 * lines, rows)
    input_grad = dot_tn(pick, total).astype(BF16).reshape(inputs.shape)
    return (hyena.reshape(output_grad.shape), input_grad, weight_grad)


def solution(mesh):
    fsdp, tp = (mesh.shape[name] for name in ("fsdp", "tp"))
    side = math.isqrt(tp // 2)
    fine = Mesh(mesh.devices.reshape(fsdp // 2, 2, side, side, 2), ("zl", "core", "x", "y", "zh"))
    f, t = ("zl", "core"), ("x", "y", "zh")
    in_specs = (P(t, None, f), P(f, None, t), P(None, None, t), P(t, None), P(t), P(t), P(None, f, t))
    out_specs = (P(None, f, t), P(t, None, f), P(f, None, t))
    return jax.shard_map(layer, mesh=fine, in_specs=in_specs, out_specs=out_specs, check_vma=False)
```

```python
import functools
import math

import jax
import jax.numpy as jnp
from jax import lax
from jax.experimental import pallas as pl
from jax.experimental.pallas import tpu as pltpu
from jax.sharding import Mesh
from jax.sharding import PartitionSpec as P

F32 = jnp.float32
BF16 = jnp.bfloat16
INTERPRET = False


def call(body, outs, *args):
    whole = pl.BlockSpec(memory_space=pltpu.VMEM)
    many = isinstance(outs, (tuple, list))
    size = sum(math.prod(a.shape) * a.dtype.itemsize for a in args)
    loose = [i for i, a in enumerate(args) if a.ndim > 1 and a.shape[-1] % 128 == 0 and a.shape[-2] % 16 == 0 and a.size >= 1 << 14]

    def spec(i):
        if args[i].shape == (1,):
            return pl.BlockSpec(memory_space=pltpu.SMEM)
        return pl.BlockSpec(memory_space=pl.ANY) if i in loose else whole

    def run(*refs):
        held, sems = refs[-1 - len(loose) : -1], refs[-1]
        rest = list(refs[: -1 - len(loose)])
        copies = [pltpu.make_async_copy(rest[i], held[j], sems.at[j]) for j, i in enumerate(loose)]
        for copy in copies:
            copy.start()
        for copy in copies:
            copy.wait()
        for j, i in enumerate(loose):
            rest[i] = held[j]
        body(*rest)

    return pl.pallas_call(
        run if loose else body,
        out_shape=outs,
        in_specs=[spec(i) for i in range(len(args))],
        out_specs=[whole] * len(outs) if many else whole,
        scratch_shapes=[pltpu.VMEM(args[i].shape, args[i].dtype) for i in loose] + [pltpu.SemaphoreType.DMA((len(loose),))] * bool(loose),
        compiler_params=pltpu.CompilerParams(vmem_limit_bytes=20 << 20),
        cost_estimate=pl.CostEstimate(flops=10**9, bytes_accessed=size, transcendentals=0),
        interpret=INTERPRET,
    )(*args)


def shape(dims, kind):
    return jax.ShapeDtypeStruct(dims, kind)


def dot(a, b):
    return jnp.dot(a, b, preferred_element_type=F32)


def dot_nt(a, b):
    return lax.dot_general(a, b, (((1,), (1,)), ((), ())), preferred_element_type=F32)


def dot_tn(a, b):
    return lax.dot_general(a, b, (((0,), (0,)), ((), ())), preferred_element_type=F32)


def bit_reversed(count):
    bits = count.bit_length() - 1
    return [int(format(i, f"0{bits}b")[::-1], 2) if bits else 0 for i in range(count)]


def row_order(pieces, members, tokens, inverse):
    rows = pieces * members * tokens
    r = lax.broadcasted_iota(jnp.int32, (rows, rows), 0)
    c = lax.broadcasted_iota(jnp.int32, (rows, rows), 1)
    if inverse:
        r, c = c, r
    member, rest = r // (pieces * tokens), r % (pieces * tokens)
    piece, token = rest // tokens, rest % tokens
    return jnp.where(c == (piece * members + member) * tokens + token, 1.0, 0.0).astype(BF16)


def token_order(half, tokens, count, inverse):
    r = lax.broadcasted_iota(jnp.int32, (count, count), 0)
    c = lax.broadcasted_iota(jnp.int32, (count, count), 1)
    if inverse:
        r, c = c, r
    piece, rest = r // (2 * tokens), r % (2 * tokens)
    side, token = rest // tokens, rest % tokens
    relative = jnp.where(side == half, 0, 1)
    return jnp.where(c == relative * (count // 2) + piece * tokens + token, 1.0, 0.0).astype(BF16)


def prepare_body(pieces, members, taps_ref, rev_ref, decay_ref, fwd_ref, bwd_ref, keep_ref, send_ref, unturn_ref):
    rows = unturn_ref.shape[0]
    tokens = rows // (pieces * members)
    turn = row_order(pieces, members, tokens, False)
    keep_ref[...] = turn[: rows // 2]
    send_ref[...] = turn[rows // 2 :]
    unturn_ref[...] = row_order(pieces, members, tokens, True)
    filters, taps = taps_ref.shape
    lag = lax.broadcasted_iota(jnp.int32, (1, taps), 1)
    back = jnp.where(lag == 0, 0, taps - lag)
    row = lax.broadcasted_iota(jnp.int32, (taps, taps), 0)
    col = lax.broadcasted_iota(jnp.int32, (taps, taps), 1)
    for n in range(filters):
        rate = -decay_ref[n : n + 1, :]
        plain = taps_ref[n : n + 1, :] * jnp.exp(rate * lag.astype(F32))
        turned = rev_ref[n : n + 1, :] * jnp.exp(rate * back.astype(F32))
        rows = slice(n * taps, (n + 1) * taps)
        for source, ref, near in ((turned, fwd_ref, col <= row), (plain, bwd_ref, col >= row)):
            ring = pltpu.roll(jnp.broadcast_to(source, (taps, taps)), 0, 1, stride=1, stride_axis=0)
            ref[rows, :taps] = jnp.where(near, ring, 0.0).astype(BF16)
            ref[rows, taps:] = jnp.where(near, 0.0, ring).astype(BF16)


def project_body(core_ref, order_ref, x_ref, own_ref, peer_ref, out_ref):
    core = core_ref[0]
    members, rows, _ = out_ref.shape
    order = order_ref[...]
    mine = dot(order, x_ref[core]).astype(BF16)
    theirs = dot(order, x_ref[1 - core]).astype(BF16)
    streams, _, channels = own_ref.shape
    for i in range(streams):
        part = (dot(mine, own_ref[i]) + dot(theirs, peer_ref[i])).astype(BF16)
        out_ref[:, :, i * channels : (i + 1) * channels] = part.reshape(members, rows, channels)


def back_body(core_ref, order_ref, *refs):
    *g_refs, own_ref, peer_ref, out_ref, turned_ref = refs
    core = core_ref[0]
    streams, _, channels = own_ref.shape
    gathered = jnp.concatenate([ref[...].reshape(-1, streams * channels) for ref in g_refs], axis=0)
    g = dot(order_ref[...], gathered).astype(BF16)
    turned_ref[...] = g
    for place, ref in ((core, own_ref), (1 - core, peer_ref)):
        total = dot_nt(g[:, :channels], ref[0])
        for i in range(1, streams):
            total = total + dot_nt(g[:, i * channels : (i + 1) * channels], ref[i])
        out_ref[place] = total.astype(BF16)


def weight_body(core_ref, x0_ref, x1_ref, g0_ref, g1_ref, own_ref, peer_ref):
    core = core_ref[0]
    streams, _, channels = own_ref.shape
    for place, ref in ((core, own_ref), (1 - core, peer_ref)):
        for i in range(streams):
            cols = slice(i * channels, (i + 1) * channels)
            ref[i] = (dot_tn(x0_ref[place], g0_ref[:, cols]) + dot_tn(x1_ref[place], g1_ref[:, cols])).astype(ref.dtype)


def later(x, border, by):
    row = lax.broadcasted_iota(jnp.int32, x.shape, 0)
    moved = pltpu.roll(x, by, 0)
    for i in range(by):
        moved = jnp.where(row == i, border[8 - by + i : 9 - by + i], moved)
    return moved


def sooner(x, border, by):
    count = x.shape[0]
    row = lax.broadcasted_iota(jnp.int32, x.shape, 0)
    moved = pltpu.roll(x, count - by, 0)
    for i in range(by):
        moved = jnp.where(row == count - by + i, border[i : i + 1], moved)
    return moved


def gate_body(tokens, f0_ref, f1_ref, tail_ref, head_ref, short_ref, up_ref, after_ref, half_ref, q_ref, k_ref, v_ref, n_ref, prod_ref, cg_ref):
    count = f0_ref.shape[0] * 2
    order = token_order(half_ref[0], tokens, count, False)
    features = dot(order, jnp.concatenate([f0_ref[...], f1_ref[...]], axis=0))
    channels = up_ref.shape[1]
    outs = (q_ref, k_ref, v_ref)
    tail = tail_ref[...].astype(F32)
    head = head_ref[...].astype(F32)
    for i in range(3):
        cols = slice(i * channels, (i + 1) * channels)
        own, border = features[:, cols], tail[:, cols]
        following, own_tail = head[:, cols], features[count - 8 :, cols]
        total = short_ref[0, i : i + 1] * own
        ahead = short_ref[0, i : i + 1] * following
        for lag in range(1, short_ref.shape[0]):
            total = total + short_ref[lag, i : i + 1] * later(own, border, lag)
            ahead = ahead + short_ref[lag, i : i + 1] * later(following, own_tail, lag)
        outs[i][...] = total
        n_ref[i] = ahead
    prod_ref[...] = (k_ref[...] * v_ref[...]).astype(BF16)
    cg_ref[:count] = (up_ref[...].astype(F32) * q_ref[...]).astype(BF16)
    first = after_ref[...].astype(F32) * n_ref[0]
    row = lax.broadcasted_iota(jnp.int32, first.shape, 0)
    cg_ref[count:] = jnp.where(row == 0, first, 0.0).astype(BF16)


def convolve(t_ref, both, rows):
    count, channels = both.shape[0] // 2, both.shape[1]
    filters = t_ref.shape[0] // count
    group = lax.broadcasted_iota(jnp.int32, (1, channels), 1) // (channels // filters)
    total = jnp.zeros((rows, channels), F32)
    for n in range(filters):
        part = dot(t_ref[n * count : n * count + rows, :], both)
        total = jnp.where(group == n, part, total)
    return total


def hyena_body(
    tokens, fwd_ref, bwd_ref, prod_ref, prev_ref, cg_ref, next_ref, q_ref, k_ref, v_ref, n_ref, up_ref, after_ref, skip_ref, short_ref, half_ref,
    out_ref, g0_ref, g1_ref,
):
    count, channels = up_ref.shape
    ahead = after_ref.shape[0]
    up, q, k, v, skip = up_ref[...].astype(F32), q_ref[...], k_ref[...], v_ref[...], skip_ref[...]
    convolved = convolve(fwd_ref, jnp.concatenate([prod_ref[...], prev_ref[...]], axis=0), count) + skip * (k * v)
    out_ref[...] = (q * convolved).astype(BF16)
    following = next_ref[...]
    back = convolve(bwd_ref, jnp.concatenate([cg_ref[:count], following[:count]], axis=0), count) + skip * (up * q)
    up_n, q_n, k_n, v_n = after_ref[...].astype(F32), n_ref[0], n_ref[1], n_ref[2]
    pad = jnp.zeros((count - ahead, channels), BF16)
    both = jnp.concatenate([(k_n * v_n).astype(BF16), pad, prod_ref[...]], axis=0)
    convolved_n = convolve(fwd_ref, both, ahead) + skip * (k_n * v_n)
    back_n = convolve(bwd_ref, jnp.concatenate([following, pad], axis=0), ahead) + skip * (up_n * q_n)
    order = token_order(half_ref[0], tokens, count, True)
    grads = ((up * convolved, up_n * convolved_n), (back * v, back_n * v_n), (back * k, back_n * k_n))
    for i, (x, border) in enumerate(grads):
        cols = slice(i * channels, (i + 1) * channels)
        total = short_ref[0, i : i + 1] * x
        for lag in range(1, short_ref.shape[0]):
            total = total + short_ref[lag, i : i + 1] * sooner(x, border, lag)
        turned = dot(order, total.astype(BF16)).astype(BF16)
        g0_ref[:, cols] = turned[: count // 2]
        g1_ref[:, cols] = turned[count // 2 :]


def swap(x, axis, by=1):
    return lax.ppermute(x, axis, [(i, i ^ by) for i in range(lax.axis_size(axis))])


def shifted(x, by):
    axis = ("zl", "core")
    count = lax.axis_size("zl") * lax.axis_size("core")
    return lax.ppermute(x, axis, [(i, i + by) for i in range(count) if 0 <= i + by < count])


def line_scatter(keep, send):
    count, by = keep.shape[0], 1
    while True:
        got = swap(send, "zl", by)
        if count == 1:
            return (keep[0].astype(F32) + got[0].astype(F32)).astype(BF16)
        half = count // 2
        send = (keep[half:].astype(F32) + got[half:].astype(F32)).astype(BF16)
        keep = (keep[:half].astype(F32) + got[:half].astype(F32)).astype(BF16)
        count, by = half, by * 2


def line_gather(x):
    parts = [x[None]]
    by = lax.axis_size("zl") // 2
    while by:
        so_far = jnp.concatenate(parts, axis=0) if len(parts) > 1 else parts[0]
        parts.append(swap(so_far, "zl", by))
        by //= 2
    return parts


def layer(inputs, featurizer, short_filter, long_filter, decay_rate, skip_gain, output_grad):
    tokens, blocks, rows = inputs.shape
    members = lax.axis_size("zl")
    pieces = lax.axis_size("x") * lax.axis_size("y")
    lines = members * tokens
    channels = featurizer.shape[2]
    wide = 3 * channels
    count = output_grad.shape[0]
    zl, core, zh = lax.axis_index("zl"), lax.axis_index("core"), lax.axis_index("zh")
    here = core.astype(jnp.int32).reshape(1)
    half = zh.astype(jnp.int32).reshape(1)

    order = jnp.array(bit_reversed(members), jnp.int32) ^ zl
    block = (order[None, :] * 2 + jnp.arange(2, dtype=jnp.int32)[:, None]).reshape(-1, 1)
    source = (jnp.arange(tokens, dtype=jnp.int32)[None, :] * blocks + block).reshape(-1, 1)
    pick = (source == jnp.arange(tokens * blocks, dtype=jnp.int32)[None, :]).astype(BF16)
    local = dot(pick, inputs.reshape(tokens * blocks, rows)).astype(BF16).reshape(2, 1, lines, rows)

    def exchange(x):
        x = lax.all_to_all(x.reshape(2 * pieces, lines, rows), ("core", "x", "y"), 0, 0, tiled=True)
        return x.reshape(2, pieces, lines, rows)

    def spread(x):
        return exchange(jnp.broadcast_to(x, (2, pieces, lines, rows))).reshape(2, pieces * lines, rows)

    x_near = spread(local)
    upstream = output_grad.reshape(count, channels)
    after = shifted(upstream[:16], -1)
    far = swap(local, "zh", 1)
    w_own = featurizer.transpose(1, 0, 2)
    w_peer = swap(w_own, "core", 1)
    rolled = jnp.roll(long_filter[:, ::-1], 1, axis=1)
    matrix = shape((long_filter.shape[0] * count, 2 * count), BF16)
    oblong = shape((pieces * lines // 2, pieces * lines), BF16)
    square = shape((pieces * lines, pieces * lines), BF16)
    t_fwd, t_bwd, turn_keep, turn_send, unturn = call(
        functools.partial(prepare_body, pieces, members),
        (matrix, matrix, oblong, oblong, square),
        long_filter, rolled, decay_rate[:, None],
    )

    part_shape = shape((members // 2, pieces * tokens, wide), BF16)

    def project(x):
        send = call(project_body, part_shape, here, turn_send, x, w_own, w_peer)
        keep = call(project_body, part_shape, here, turn_keep, x, w_own, w_peer)
        return line_scatter(keep, send)

    f_near = project(x_near)
    x_far = spread(far)
    f_far = project(x_far)
    tail = shifted(jnp.where(zh == 1, f_near[-8:], f_far[-8:]), 1)
    head = shifted(jnp.where(zh == 0, f_near[:16], f_far[:16]), -1)
    plane = shape((count, channels), F32)
    thin = shape((count, channels), BF16)
    longer = shape((count + 16, channels), BF16)
    q, k, v, ahead, prod, cg = call(
        functools.partial(gate_body, tokens),
        (plane, plane, plane, shape((3, 16, channels), F32), thin, longer),
        f_near, f_far, tail, head, short_filter, upstream, after, half,
    )
    prev, nxt = shifted(prod, 1), shifted(cg, -1)
    piece_shape = shape((count // 2, wide), BF16)
    hyena, g_near, g_far = call(
        functools.partial(hyena_body, tokens),
        (thin, piece_shape, piece_shape),
        t_fwd, t_bwd, prod, prev, cg, nxt, q, k, v, ahead, upstream, after, skip_gain[None, :], short_filter, half,
    )
    back_shapes = (shape((2, pieces * lines, rows), BF16), shape((pieces * lines, wide), BF16))

    def collect(x):
        x = exchange(x)
        return jnp.sum(x.astype(F32), axis=1)

    d_far, turned_far = call(back_body, back_shapes, here, unturn, *line_gather(g_far), w_own, w_peer)
    sent = swap(collect(d_far).astype(BF16), "zh", 1)
    d_near, turned_near = call(back_body, back_shapes, here, unturn, *line_gather(g_near), w_own, w_peer)
    weight_shape = (3, rows, channels)
    w_grad, w_far = call(weight_body, (shape(weight_shape, F32), shape(weight_shape, BF16)), here, x_near, x_far, turned_near, turned_far)
    weight_grad = (w_grad + swap(w_far, "core").astype(F32)).astype(BF16).transpose(1, 0, 2)
    total = (collect(d_near) + sent.astype(F32)).astype(BF16).reshape(2 * lines, rows)
    input_grad = dot_tn(pick, total).astype(BF16).reshape(inputs.shape)
    return (hyena.reshape(output_grad.shape), input_grad, weight_grad)


def solution(mesh):
    fsdp, tp = (mesh.shape[name] for name in ("fsdp", "tp"))
    side = math.isqrt(tp // 2)
    fine = Mesh(mesh.devices.reshape(fsdp // 2, 2, side, side, 2), ("zl", "core", "x", "y", "zh"))
    f, t = ("zl", "core"), ("x", "y", "zh")
    in_specs = (P(t, None, f), P(f, None, t), P(None, None, t), P(t, None), P(t), P(t), P(None, f, t))
    out_specs = (P(None, f, t), P(t, None, f), P(f, None, t))
    return jax.shard_map(layer, mesh=fine, in_specs=in_specs, out_specs=out_specs, check_vma=False)
```

```python
import functools
import math

import jax
import jax.numpy as jnp
from jax import lax
from jax.experimental import pallas as pl
from jax.experimental.pallas import tpu as pltpu
from jax.sharding import Mesh
from jax.sharding import PartitionSpec as P

F32 = jnp.float32
BF16 = jnp.bfloat16
INTERPRET = False


def call(body, outs, *args):
    whole = pl.BlockSpec(memory_space=pltpu.VMEM)
    many = isinstance(outs, (tuple, list))
    size = sum(math.prod(a.shape) * a.dtype.itemsize for a in args)
    loose = [i for i, a in enumerate(args) if a.ndim > 1 and a.shape[-1] % 128 == 0 and a.shape[-2] % 16 == 0 and a.size >= 1 << 14]

    def spec(i):
        if args[i].shape == (1,):
            return pl.BlockSpec(memory_space=pltpu.SMEM)
        return pl.BlockSpec(memory_space=pl.ANY) if i in loose else whole

    def run(*refs):
        held, sems = refs[-1 - len(loose) : -1], refs[-1]
        rest = list(refs[: -1 - len(loose)])
        copies = [pltpu.make_async_copy(rest[i], held[j], sems.at[j]) for j, i in enumerate(loose)]
        for copy in copies:
            copy.start()
        for copy in copies:
            copy.wait()
        for j, i in enumerate(loose):
            rest[i] = held[j]
        body(*rest)

    return pl.pallas_call(
        run if loose else body,
        out_shape=outs,
        in_specs=[spec(i) for i in range(len(args))],
        out_specs=[whole] * len(outs) if many else whole,
        scratch_shapes=[pltpu.VMEM(args[i].shape, args[i].dtype) for i in loose] + [pltpu.SemaphoreType.DMA((len(loose),))] * bool(loose),
        compiler_params=pltpu.CompilerParams(vmem_limit_bytes=20 << 20),
        cost_estimate=pl.CostEstimate(flops=10**9, bytes_accessed=size, transcendentals=0),
        interpret=INTERPRET,
    )(*args)


def shape(dims, kind):
    return jax.ShapeDtypeStruct(dims, kind)


def dot(a, b):
    return jnp.dot(a, b, preferred_element_type=F32)


def dot_nt(a, b):
    return lax.dot_general(a, b, (((1,), (1,)), ((), ())), preferred_element_type=F32)


def dot_tn(a, b):
    return lax.dot_general(a, b, (((0,), (0,)), ((), ())), preferred_element_type=F32)


def bit_reversed(count):
    bits = count.bit_length() - 1
    return [int(format(i, f"0{bits}b")[::-1], 2) if bits else 0 for i in range(count)]


def row_order(pieces, members, tokens, inverse):
    rows = pieces * members * tokens
    r = lax.broadcasted_iota(jnp.int32, (rows, rows), 0)
    c = lax.broadcasted_iota(jnp.int32, (rows, rows), 1)
    if inverse:
        r, c = c, r
    member, rest = r // (pieces * tokens), r % (pieces * tokens)
    piece, token = rest // tokens, rest % tokens
    return jnp.where(c == (piece * members + member) * tokens + token, 1.0, 0.0).astype(BF16)


def token_order(half, tokens, count, inverse):
    r = lax.broadcasted_iota(jnp.int32, (count, count), 0)
    c = lax.broadcasted_iota(jnp.int32, (count, count), 1)
    if inverse:
        r, c = c, r
    piece, rest = r // (2 * tokens), r % (2 * tokens)
    side, token = rest // tokens, rest % tokens
    relative = jnp.where(side == half, 0, 1)
    return jnp.where(c == relative * (count // 2) + piece * tokens + token, 1.0, 0.0).astype(BF16)


def prepare_body(pieces, members, taps_ref, rev_ref, decay_ref, fwd_ref, bwd_ref, keep_ref, send_ref, unturn_ref):
    rows = unturn_ref.shape[0]
    tokens = rows // (pieces * members)
    turn = row_order(pieces, members, tokens, False)
    keep_ref[...] = turn[: rows // 2]
    send_ref[...] = turn[rows // 2 :]
    unturn_ref[...] = row_order(pieces, members, tokens, True)
    filters, taps = taps_ref.shape
    lag = lax.broadcasted_iota(jnp.int32, (1, taps), 1)
    back = jnp.where(lag == 0, 0, taps - lag)
    row = lax.broadcasted_iota(jnp.int32, (taps, taps), 0)
    col = lax.broadcasted_iota(jnp.int32, (taps, taps), 1)
    for n in range(filters):
        rate = -decay_ref[n : n + 1, :]
        plain = taps_ref[n : n + 1, :] * jnp.exp(rate * lag.astype(F32))
        turned = rev_ref[n : n + 1, :] * jnp.exp(rate * back.astype(F32))
        rows = slice(n * taps, (n + 1) * taps)
        for source, ref, near in ((turned, fwd_ref, col <= row), (plain, bwd_ref, col >= row)):
            ring = pltpu.roll(jnp.broadcast_to(source, (taps, taps)), 0, 1, stride=1, stride_axis=0)
            ref[rows, :taps] = jnp.where(near, ring, 0.0).astype(BF16)
            ref[rows, taps:] = jnp.where(near, 0.0, ring).astype(BF16)


def project_body(core_ref, order_ref, x_ref, own_ref, peer_ref, out_ref):
    core = core_ref[0]
    members, rows, _ = out_ref.shape
    order = order_ref[...]
    x = jnp.concatenate([dot(order, x_ref[place]).astype(BF16) for place in (core, 1 - core)], axis=1)
    streams, _, channels = own_ref.shape
    for i in range(streams):
        part = dot(x, jnp.concatenate([own_ref[i], peer_ref[i]], axis=0)).astype(BF16)
        out_ref[:, :, i * channels : (i + 1) * channels] = part.reshape(members, rows, channels)


def back_body(core_ref, order_ref, *refs):
    *g_refs, own_ref, peer_ref, out_ref, turned_ref = refs
    core = core_ref[0]
    streams, _, channels = own_ref.shape
    gathered = jnp.concatenate([ref[...].reshape(-1, streams * channels) for ref in g_refs], axis=0)
    g = dot(order_ref[...], gathered).astype(BF16)
    turned_ref[...] = g
    for place, ref in ((core, own_ref), (1 - core, peer_ref)):
        weights = jnp.concatenate([ref[i] for i in range(streams)], axis=1)
        out_ref[place] = dot_nt(g, weights).astype(BF16)


def weight_body(core_ref, x0_ref, x1_ref, g0_ref, g1_ref, own_ref, peer_ref):
    core = core_ref[0]
    streams, _, channels = own_ref.shape
    for place, ref in ((core, own_ref), (1 - core, peer_ref)):
        for i in range(streams):
            cols = slice(i * channels, (i + 1) * channels)
            ref[i] = (dot_tn(x0_ref[place], g0_ref[:, cols]) + dot_tn(x1_ref[place], g1_ref[:, cols])).astype(ref.dtype)


def later(x, border, by):
    row = lax.broadcasted_iota(jnp.int32, x.shape, 0)
    moved = pltpu.roll(x, by, 0)
    for i in range(by):
        moved = jnp.where(row == i, border[8 - by + i : 9 - by + i], moved)
    return moved


def sooner(x, border, by):
    count = x.shape[0]
    row = lax.broadcasted_iota(jnp.int32, x.shape, 0)
    moved = pltpu.roll(x, count - by, 0)
    for i in range(by):
        moved = jnp.where(row == count - by + i, border[i : i + 1], moved)
    return moved


def gate_body(tokens, f0_ref, f1_ref, tail_ref, head_ref, short_ref, up_ref, after_ref, half_ref, q_ref, k_ref, v_ref, n_ref, prod_ref, cg_ref):
    count = f0_ref.shape[0] * 2
    order = token_order(half_ref[0], tokens, count, False)
    features = dot(order, jnp.concatenate([f0_ref[...], f1_ref[...]], axis=0))
    channels = up_ref.shape[1]
    outs = (q_ref, k_ref, v_ref)
    tail = tail_ref[...].astype(F32)
    head = head_ref[...].astype(F32)
    for i in range(3):
        cols = slice(i * channels, (i + 1) * channels)
        own, border = features[:, cols], tail[:, cols]
        following, own_tail = head[:, cols], features[count - 8 :, cols]
        total = short_ref[0, i : i + 1] * own
        ahead = short_ref[0, i : i + 1] * following
        for lag in range(1, short_ref.shape[0]):
            total = total + short_ref[lag, i : i + 1] * later(own, border, lag)
            ahead = ahead + short_ref[lag, i : i + 1] * later(following, own_tail, lag)
        outs[i][...] = total
        n_ref[i] = ahead
    prod_ref[...] = (k_ref[...] * v_ref[...]).astype(BF16)
    cg_ref[:count] = (up_ref[...].astype(F32) * q_ref[...]).astype(BF16)
    first = after_ref[...].astype(F32) * n_ref[0]
    row = lax.broadcasted_iota(jnp.int32, first.shape, 0)
    cg_ref[count:] = jnp.where(row == 0, first, 0.0).astype(BF16)


def convolve(t_ref, both, rows):
    count, channels = both.shape[0] // 2, both.shape[1]
    filters = t_ref.shape[0] // count
    group = lax.broadcasted_iota(jnp.int32, (1, channels), 1) // (channels // filters)
    total = jnp.zeros((rows, channels), F32)
    for n in range(filters):
        part = dot(t_ref[n * count : n * count + rows, :], both)
        total = jnp.where(group == n, part, total)
    return total


def hyena_body(
    tokens, fwd_ref, bwd_ref, prod_ref, prev_ref, cg_ref, next_ref, q_ref, k_ref, v_ref, n_ref, up_ref, after_ref, skip_ref, short_ref, half_ref,
    out_ref, g0_ref, g1_ref,
):
    count, channels = up_ref.shape
    ahead = after_ref.shape[0]
    up, q, k, v, skip = up_ref[...].astype(F32), q_ref[...], k_ref[...], v_ref[...], skip_ref[...]
    convolved = convolve(fwd_ref, jnp.concatenate([prod_ref[...], prev_ref[...]], axis=0), count) + skip * (k * v)
    out_ref[...] = (q * convolved).astype(BF16)
    following = next_ref[...]
    back = convolve(bwd_ref, jnp.concatenate([cg_ref[:count], following[:count]], axis=0), count) + skip * (up * q)
    up_n, q_n, k_n, v_n = after_ref[...].astype(F32), n_ref[0], n_ref[1], n_ref[2]
    pad = jnp.zeros((count - ahead, channels), BF16)
    both = jnp.concatenate([(k_n * v_n).astype(BF16), pad, prod_ref[...]], axis=0)
    convolved_n = convolve(fwd_ref, both, ahead) + skip * (k_n * v_n)
    back_n = convolve(bwd_ref, jnp.concatenate([following, pad], axis=0), ahead) + skip * (up_n * q_n)
    order = token_order(half_ref[0], tokens, count, True)
    grads = ((up * convolved, up_n * convolved_n), (back * v, back_n * v_n), (back * k, back_n * k_n))
    for i, (x, border) in enumerate(grads):
        cols = slice(i * channels, (i + 1) * channels)
        total = short_ref[0, i : i + 1] * x
        for lag in range(1, short_ref.shape[0]):
            total = total + short_ref[lag, i : i + 1] * sooner(x, border, lag)
        turned = dot(order, total.astype(BF16)).astype(BF16)
        g0_ref[:, cols] = turned[: count // 2]
        g1_ref[:, cols] = turned[count // 2 :]


def swap(x, axis, by=1):
    return lax.ppermute(x, axis, [(i, i ^ by) for i in range(lax.axis_size(axis))])


def shifted(x, by):
    axis = ("zl", "core")
    count = lax.axis_size("zl") * lax.axis_size("core")
    return lax.ppermute(x, axis, [(i, i + by) for i in range(count) if 0 <= i + by < count])


def line_scatter(keep, send):
    count, by = keep.shape[0], 1
    while True:
        got = swap(send, "zl", by)
        if count == 1:
            return (keep[0].astype(F32) + got[0].astype(F32)).astype(BF16)
        half = count // 2
        send = (keep[half:].astype(F32) + got[half:].astype(F32)).astype(BF16)
        keep = (keep[:half].astype(F32) + got[:half].astype(F32)).astype(BF16)
        count, by = half, by * 2


def line_gather(x):
    parts = [x[None]]
    by = lax.axis_size("zl") // 2
    while by:
        so_far = jnp.concatenate(parts, axis=0) if len(parts) > 1 else parts[0]
        parts.append(swap(so_far, "zl", by))
        by //= 2
    return parts


def layer(inputs, featurizer, short_filter, long_filter, decay_rate, skip_gain, output_grad):
    tokens, blocks, rows = inputs.shape
    members = lax.axis_size("zl")
    pieces = lax.axis_size("x") * lax.axis_size("y")
    lines = members * tokens
    channels = featurizer.shape[2]
    wide = 3 * channels
    count = output_grad.shape[0]
    zl, core, zh = lax.axis_index("zl"), lax.axis_index("core"), lax.axis_index("zh")
    here = core.astype(jnp.int32).reshape(1)
    half = zh.astype(jnp.int32).reshape(1)

    order = jnp.array(bit_reversed(members), jnp.int32) ^ zl
    block = (order[None, :] * 2 + jnp.arange(2, dtype=jnp.int32)[:, None]).reshape(-1, 1)
    source = (jnp.arange(tokens, dtype=jnp.int32)[None, :] * blocks + block).reshape(-1, 1)
    pick = (source == jnp.arange(tokens * blocks, dtype=jnp.int32)[None, :]).astype(BF16)
    local = dot(pick, inputs.reshape(tokens * blocks, rows)).astype(BF16).reshape(2, 1, lines, rows)

    def exchange(x):
        x = lax.all_to_all(x.reshape(2 * pieces, lines, rows), ("core", "x", "y"), 0, 0, tiled=True)
        return x.reshape(2, pieces, lines, rows)

    def spread(x):
        return exchange(jnp.broadcast_to(x, (2, pieces, lines, rows))).reshape(2, pieces * lines, rows)

    x_near = spread(local)
    upstream = output_grad.reshape(count, channels)
    after = shifted(upstream[:16], -1)
    far = swap(local, "zh", 1)
    w_own = featurizer.transpose(1, 0, 2)
    w_peer = swap(w_own, "core", 1)
    rolled = jnp.roll(long_filter[:, ::-1], 1, axis=1)
    matrix = shape((long_filter.shape[0] * count, 2 * count), BF16)
    oblong = shape((pieces * lines // 2, pieces * lines), BF16)
    square = shape((pieces * lines, pieces * lines), BF16)
    t_fwd, t_bwd, turn_keep, turn_send, unturn = call(
        functools.partial(prepare_body, pieces, members),
        (matrix, matrix, oblong, oblong, square),
        long_filter, rolled, decay_rate[:, None],
    )

    part_shape = shape((members // 2, pieces * tokens, wide), BF16)

    def project(x):
        send = call(project_body, part_shape, here, turn_send, x, w_own, w_peer)
        keep = call(project_body, part_shape, here, turn_keep, x, w_own, w_peer)
        return line_scatter(keep, send)

    f_near = project(x_near)
    x_far = spread(far)
    f_far = project(x_far)
    tail = shifted(jnp.where(zh == 1, f_near[-8:], f_far[-8:]), 1)
    head = shifted(jnp.where(zh == 0, f_near[:16], f_far[:16]), -1)
    plane = shape((count, channels), F32)
    thin = shape((count, channels), BF16)
    longer = shape((count + 16, channels), BF16)
    q, k, v, ahead, prod, cg = call(
        functools.partial(gate_body, tokens),
        (plane, plane, plane, shape((3, 16, channels), F32), thin, longer),
        f_near, f_far, tail, head, short_filter, upstream, after, half,
    )
    prev, nxt = shifted(prod, 1), shifted(cg, -1)
    piece_shape = shape((count // 2, wide), BF16)
    hyena, g_near, g_far = call(
        functools.partial(hyena_body, tokens),
        (thin, piece_shape, piece_shape),
        t_fwd, t_bwd, prod, prev, cg, nxt, q, k, v, ahead, upstream, after, skip_gain[None, :], short_filter, half,
    )
    back_shapes = (shape((2, pieces * lines, rows), BF16), shape((pieces * lines, wide), BF16))

    def collect(x):
        x = exchange(x)
        return jnp.sum(x.astype(F32), axis=1)

    d_far, turned_far = call(back_body, back_shapes, here, unturn, *line_gather(g_far), w_own, w_peer)
    sent = swap(collect(d_far).astype(BF16), "zh", 1)
    d_near, turned_near = call(back_body, back_shapes, here, unturn, *line_gather(g_near), w_own, w_peer)
    weight_shape = (3, rows, channels)
    w_grad, w_far = call(weight_body, (shape(weight_shape, F32), shape(weight_shape, BF16)), here, x_near, x_far, turned_near, turned_far)
    weight_grad = (w_grad + swap(w_far, "core").astype(F32)).astype(BF16).transpose(1, 0, 2)
    total = (collect(d_near) + sent.astype(F32)).astype(BF16).reshape(2 * lines, rows)
    input_grad = dot_tn(pick, total).astype(BF16).reshape(inputs.shape)
    return (hyena.reshape(output_grad.shape), input_grad, weight_grad)


def solution(mesh):
    fsdp, tp = (mesh.shape[name] for name in ("fsdp", "tp"))
    side = math.isqrt(tp // 2)
    fine = Mesh(mesh.devices.reshape(fsdp // 2, 2, side, side, 2), ("zl", "core", "x", "y", "zh"))
    f, t = ("zl", "core"), ("x", "y", "zh")
    in_specs = (P(t, None, f), P(f, None, t), P(None, None, t), P(t, None), P(t), P(t), P(None, f, t))
    out_specs = (P(None, f, t), P(t, None, f), P(f, None, t))
    return jax.shard_map(layer, mesh=fine, in_specs=in_specs, out_specs=out_specs, check_vma=False)
```
